32 devices in a mesh: dp: 4 (over x, core), fsdp: 8 (over z, y).
Axes of the slice: x: 2, y: 2, z: 4, core: 2. Of those that a mesh axis runs over, the one named last changes fastest.
Arguments:
- tokens: bfloat16 [18432, 576], P(('dp', 'fsdp')), may hold values from -6 to 6
- cotangent: bfloat16 [18432, 576], P(('dp', 'fsdp')), may hold values from -6 to 6
- w_query: bfloat16 [576, 576], P(None, 'fsdp'), may hold values from -0.25 to 0.25
- key_projection_weight: bfloat16 [576, 192], P(None, 'fsdp'), may hold values from -0.25 to 0.25
- value_projection_weight: bfloat16 [576, 192], P(None, 'fsdp'), may hold values from -0.25 to 0.25
- output_projection_weight: bfloat16 [576, 576], P(None, 'fsdp'), may hold values from -0.75 to 0.75
- w_gate: bfloat16 [576, 1536], P(None, 'fsdp'), may hold values from -0.25 to 0.25
- w_up: bfloat16 [576, 1536], P(None, 'fsdp'), may hold values from -0.25 to 0.25
- w_down: bfloat16 [1536, 576], P(None, 'fsdp'), may hold values from -0.21875 to 0.21875
- gain_attn: bfloat16 [576], P('fsdp'), may hold values from 0.099609375 to 1.8984375
- gain_mlp: bfloat16 [576], P('fsdp'), may hold values from 0.099609375 to 1.8984375
Outputs:
- output: bfloat16 [18432, 576], P(('dp', 'fsdp'))
- grad_tokens: bfloat16 [18432, 576], P(('dp', 'fsdp'))
- grad_query: float32 [576, 576], P(None, 'fsdp')
- grad_key: float32 [576, 192], P(None, 'fsdp')
- grad_value: float32 [576, 192], P(None, 'fsdp')
- grad_out: float32 [576, 576], P(None, 'fsdp')
- grad_gate: float32 [576, 1536], P(None, 'fsdp')
- grad_up: float32 [576, 1536], P(None, 'fsdp')
- grad_down: float32 [1536, 576], P(None, 'fsdp')
- grad_gain_attn: float32 [576], P('fsdp')
- grad_gain_mlp: float32 [576], P('fsdp')
The draws below stay inside these ranges and needn't reach their ends.
All inputs are finite; a program needn't handle non-finite values.
Results may differ from the reference program's by a relative error of at most 0.017.
Values may be sent and summed in bfloat16 or wider, within the bound.
No kernel may reach another device: no remote copies, remote signals or barrier semaphores. Data moves between devices by JAX's collectives and lax.ppermute only.
A program may use at most 128 MiB of HBM per device.

```python
import jax
import jax.numpy as jnp
from jax import lax

MODEL_WIDTH = 576
QUERY_HEADS = 9
KEY_VALUE_HEADS = 3
HEAD_SIZE = 64
FF = 1536
SEQUENCE_LENGTH = 192
TOKENS = 18432


def spiked(values, own_key, source, target, blocks, factor):
    def block_of(dim):
        return (jnp.arange(values.shape[dim]) // (values.shape[dim] // blocks)).reshape((-1,) + (1,) * (values.ndim - 1 - dim))

    first = jax.random.permutation(own_key, blocks)[block_of(target)]
    far = (block_of(target) + blocks // 2) % blocks
    return jnp.where((block_of(source) == first) | (block_of(source) == far), factor * values, values)


def block_scale(own_key, extent, cuts, low, high):
    def one(axis_at, shards_of):
        steps = jax.random.uniform(jax.random.fold_in(jax.random.fold_in(own_key, 6), axis_at), (shards_of,), jnp.float32, low / len(cuts), high / len(cuts))
        return jnp.repeat(jnp.exp(steps), extent[axis_at] // shards_of).reshape((-1,) + (1,) * (len(extent) - axis_at - 1))

    loudness = one(*cuts[0])
    for cut in cuts[1:]:
        loudness = loudness * one(*cut)
    return loudness


def bell_draw(key, dims, width, reach, cuts=(), kind=jnp.bfloat16):
    factor_of = block_scale(key, dims, cuts, -0.22, 0.18) if cuts else 1.0
    result = jax.random.normal(key, dims, jnp.float32) * width * factor_of
    return jnp.minimum(jnp.maximum(result, -reach), reach).astype(kind)


def heavy_noise(stream_key, dims, deviation, limit, pieces, heavy, held_as=jnp.bfloat16):
    drawn = deviation * jax.random.normal(stream_key, dims, jnp.float32)
    if pieces:
        drawn = drawn * block_scale(stream_key, dims, pieces, -0.22, 0.18)
    return jnp.clip(spiked(drawn, jax.random.fold_in(stream_key, 3), *heavy), -limit, limit).astype(held_as)


def setup_inputs(seed: int = 0) -> dict:
    arg_keys = jax.random.split(jax.random.key(seed), 12)
    tokens = bell_draw(arg_keys[0], (TOKENS, MODEL_WIDTH), 1.0, 6.0, ((0, 32),))
    cotangent = heavy_noise(arg_keys[1], (TOKENS, MODEL_WIDTH), 1.0, 6.0, ((0, 32),), (0, 1, 32, 2.75))
    w_query = bell_draw(arg_keys[2], (MODEL_WIDTH, QUERY_HEADS * HEAD_SIZE), MODEL_WIDTH ** -0.5, 0.25, ((1, 8),))
    key_projection_weight = bell_draw(arg_keys[3], (MODEL_WIDTH, KEY_VALUE_HEADS * HEAD_SIZE), MODEL_WIDTH ** -0.5, 0.25, ((1, 8),))
    value_projection_weight = bell_draw(arg_keys[4], (MODEL_WIDTH, KEY_VALUE_HEADS * HEAD_SIZE), MODEL_WIDTH ** -0.5, 0.25, ((1, 8),))
    output_projection_weight = bell_draw(arg_keys[5], (QUERY_HEADS * HEAD_SIZE, MODEL_WIDTH), (QUERY_HEADS * HEAD_SIZE // 8) ** -0.5, 0.75, ((1, 8),))
    w_gate = bell_draw(arg_keys[6], (MODEL_WIDTH, FF), MODEL_WIDTH ** -0.5, 0.25, ((1, 8),))
    w_up = bell_draw(arg_keys[7], (MODEL_WIDTH, FF), MODEL_WIDTH ** -0.5, 0.25, ((1, 8),))
    w_down = bell_draw(arg_keys[8], (FF, MODEL_WIDTH), (FF // 2) ** -0.5, 0.21875, ((1, 8),))
    gain_attn = jnp.clip(1.0 + 0.18 * jax.random.normal(arg_keys[9], (MODEL_WIDTH,), jnp.float32), 0.099609375, 1.8984375).astype(jnp.bfloat16)
    gain_mlp = jnp.clip(1.0 + 0.18 * jax.random.normal(arg_keys[10], (MODEL_WIDTH,), jnp.float32), 0.099609375, 1.8984375).astype(jnp.bfloat16)
    return dict(tokens=tokens, cotangent=cotangent, w_query=w_query, key_projection_weight=key_projection_weight, value_projection_weight=value_projection_weight, output_projection_weight=output_projection_weight, w_gate=w_gate, w_up=w_up, w_down=w_down, gain_attn=gain_attn, gain_mlp=gain_mlp)


EPS_NORM = 1e-05
ROPE_BASE = 100000.0

def matrix_product(left, right):
    return jnp.dot(left, right, preferred_element_type=jnp.float32)

def einsum_f32(form, left, right):
    return jnp.einsum(form, left.astype(jnp.float32), right.astype(jnp.float32))

def rope_tables(length, head):
    half = head // 2
    position = jnp.arange(length).astype(jnp.float32)
    freqs = ROPE_BASE ** (-(jnp.arange(half).astype(jnp.float32) * 2.0 / head))
    angles = position[:, None] * freqs[None, :]
    return (jnp.cos(angles)[:, None, :], jnp.sin(angles)[:, None, :])

def apply_rotary_embedding(value_rows, cosine_table, sine_table):
    half = value_rows.shape[-1] // 2
    first = value_rows[..., :half]
    second = value_rows[..., half:]
    return jnp.concatenate([first * cosine_table - second * sine_table, second * cosine_table + first * sine_table], -1)

def reverse_rotary_embedding(value_rows, cosine_table, sine_table):
    half = value_rows.shape[-1] // 2
    first = value_rows[..., :half]
    second = value_rows[..., half:]
    return jnp.concatenate([first * cosine_table + second * sine_table, second * cosine_table - first * sine_table], -1)

def causal_mask():
    places = jnp.arange(SEQUENCE_LENGTH)
    return places[:, None] >= places[None, :]

def make_probs(query_rows, key_rows, log_total, allowed):
    scores = einsum_f32('nqkgd,nskd->nkgqs', query_rows, key_rows) * HEAD_SIZE ** (-0.5)
    return jnp.where(allowed, jnp.exp(scores - log_total), 0.0).astype(jnp.bfloat16)

def layer_forward(tokens, weights, cosine_table, sine_table):
    w_query, key_projection_weight, value_projection_weight, output_projection_weight, w_gate, w_up, w_down, gain_attn, gain_mlp = weights
    token_rows = tokens.shape[0]
    sequence_count = token_rows // SEQUENCE_LENGTH
    query_group_size = QUERY_HEADS // KEY_VALUE_HEADS
    allowed = causal_mask()
    xfull = tokens.astype(jnp.float32)
    inv_one = lax.rsqrt(lax.optimization_barrier(jnp.mean(xfull * xfull, -1, keepdims=True)) + EPS_NORM)
    first_normed_input = (xfull * inv_one * gain_attn.astype(jnp.float32)).astype(jnp.bfloat16)
    query_rows = apply_rotary_embedding(matrix_product(first_normed_input, w_query).reshape(sequence_count, SEQUENCE_LENGTH, QUERY_HEADS, HEAD_SIZE), cosine_table, sine_table).astype(jnp.bfloat16)
    key_rows = apply_rotary_embedding(matrix_product(first_normed_input, key_projection_weight).reshape(sequence_count, SEQUENCE_LENGTH, KEY_VALUE_HEADS, HEAD_SIZE), cosine_table, sine_table).astype(jnp.bfloat16)
    value_rows = matrix_product(first_normed_input, value_projection_weight).reshape(sequence_count, SEQUENCE_LENGTH, KEY_VALUE_HEADS, HEAD_SIZE).astype(jnp.bfloat16)
    grouped_queries = query_rows.reshape(sequence_count, SEQUENCE_LENGTH, KEY_VALUE_HEADS, query_group_size, HEAD_SIZE)
    scores = einsum_f32('nqkgd,nskd->nkgqs', grouped_queries, key_rows) * HEAD_SIZE ** (-0.5)
    expo = jnp.where(allowed, jnp.exp(jnp.where(allowed, scores, 0.0)), 0.0)
    log_total = jnp.log(lax.optimization_barrier(jnp.sum(expo, -1, keepdims=True)))
    probs = jnp.where(allowed, jnp.exp(scores - log_total), 0.0).astype(jnp.bfloat16)
    attention_output = einsum_f32('nkgqs,nskd->nqkgd', probs, value_rows).reshape(token_rows, QUERY_HEADS * HEAD_SIZE).astype(jnp.bfloat16)
    middle = xfull + matrix_product(attention_output, output_projection_weight)
    inv_two = lax.rsqrt(lax.optimization_barrier(jnp.mean(middle * middle, -1, keepdims=True)) + EPS_NORM)
    normed_two = (middle * inv_two * gain_mlp.astype(jnp.float32)).astype(jnp.bfloat16)
    gate = matrix_product(normed_two, w_gate)
    upper = matrix_product(normed_two, w_up)
    hidden = (jax.nn.silu(gate) * upper).astype(jnp.bfloat16)
    output = (middle + matrix_product(hidden, w_down)).astype(jnp.bfloat16)
    saved = (xfull, inv_one, first_normed_input, grouped_queries, key_rows, value_rows, log_total, attention_output, middle, inv_two, normed_two, gate, upper, hidden)
    return (output, saved)

def layer_backward(cotangent, saved, weights, cosine_table, sine_table):
    w_query, key_projection_weight, value_projection_weight, output_projection_weight, w_gate, w_up, w_down, gain_attn, gain_mlp = weights
    xfull, inv_one, first_normed_input, grouped_queries, key_rows, value_rows, log_total, attention_output, middle, inv_two, normed_two, gate, upper, hidden = saved
    token_rows = cotangent.shape[0]
    sequence_count = token_rows // SEQUENCE_LENGTH
    query_group_size = QUERY_HEADS // KEY_VALUE_HEADS
    allowed = causal_mask()
    grad_down = matrix_product(hidden.T, cotangent)
    dhidden = matrix_product(cotangent, w_down.T)
    sigma = jax.nn.sigmoid(gate)
    dgate = (dhidden * upper * sigma * (1.0 + gate * (1.0 - sigma))).astype(jnp.bfloat16)
    dupper = (dhidden * gate * sigma).astype(jnp.bfloat16)
    grad_gate = matrix_product(normed_two.T, dgate)
    grad_up = matrix_product(normed_two.T, dupper)
    dnormed_two = matrix_product(dgate, w_gate.T) + matrix_product(dupper, w_up.T)
    unit_two = middle * inv_two
    grad_gain_mlp = lax.optimization_barrier(jnp.sum(dnormed_two * unit_two, 0))
    scaled_two = dnormed_two * gain_mlp.astype(jnp.float32)
    dmiddle = inv_two * (scaled_two - unit_two * lax.optimization_barrier(jnp.mean(scaled_two * unit_two, -1, keepdims=True))) + cotangent.astype(jnp.float32)
    middle_gradient_block = dmiddle.astype(jnp.bfloat16)
    grad_out = matrix_product(attention_output.T, middle_gradient_block)
    attention_gradient = matrix_product(middle_gradient_block, output_projection_weight.T).astype(jnp.bfloat16).reshape(sequence_count, SEQUENCE_LENGTH, KEY_VALUE_HEADS, query_group_size, HEAD_SIZE)
    probs = make_probs(grouped_queries, key_rows, log_total, allowed)
    softmax_correction = lax.optimization_barrier(jnp.sum(attention_gradient.astype(jnp.float32) * attention_output.reshape(sequence_count, SEQUENCE_LENGTH, KEY_VALUE_HEADS, query_group_size, HEAD_SIZE).astype(jnp.float32), -1))
    softmax_correction = jnp.transpose(softmax_correction, (0, 2, 3, 1))[..., None]
    value_gradient_rows = einsum_f32('nkgqs,nqkgd->nskd', probs, attention_gradient)
    dprobs = einsum_f32('nqkgd,nskd->nkgqs', attention_gradient, value_rows)
    dscores = (probs.astype(jnp.float32) * (dprobs - softmax_correction) * HEAD_SIZE ** (-0.5)).astype(jnp.bfloat16)
    dqueries = einsum_f32('nkgqs,nskd->nqkgd', dscores, key_rows).reshape(sequence_count, SEQUENCE_LENGTH, QUERY_HEADS, HEAD_SIZE)
    key_gradient_rows = einsum_f32('nkgqs,nqkgd->nskd', dscores, grouped_queries)
    dq_flat = reverse_rotary_embedding(dqueries, cosine_table, sine_table).reshape(token_rows, QUERY_HEADS * HEAD_SIZE).astype(jnp.bfloat16)
    key_gradient_flat = reverse_rotary_embedding(key_gradient_rows, cosine_table, sine_table).reshape(token_rows, KEY_VALUE_HEADS * HEAD_SIZE).astype(jnp.bfloat16)
    value_gradient_flat = value_gradient_rows.reshape(token_rows, KEY_VALUE_HEADS * HEAD_SIZE).astype(jnp.bfloat16)
    grad_query = matrix_product(first_normed_input.T, dq_flat)
    grad_key = matrix_product(first_normed_input.T, key_gradient_flat)
    grad_value = matrix_product(first_normed_input.T, value_gradient_flat)
    dnormed_one = matrix_product(dq_flat, w_query.T) + matrix_product(key_gradient_flat, key_projection_weight.T) + matrix_product(value_gradient_flat, value_projection_weight.T)
    unit_one = xfull * inv_one
    grad_gain_attn = lax.optimization_barrier(jnp.sum(dnormed_one * unit_one, 0))
    scaled_one = dnormed_one * gain_attn.astype(jnp.float32)
    grad_tokens = (inv_one * (scaled_one - unit_one * lax.optimization_barrier(jnp.mean(scaled_one * unit_one, -1, keepdims=True))) + dmiddle).astype(jnp.bfloat16)
    grads = (grad_query, grad_key, grad_value, grad_out, grad_gate, grad_up, grad_down, grad_gain_attn, grad_gain_mlp)
    return (grad_tokens, grads)

def reference(tokens, cotangent, w_query, key_projection_weight, value_projection_weight, output_projection_weight, w_gate, w_up, w_down, gain_attn, gain_mlp):
    weights = (w_query, key_projection_weight, value_projection_weight, output_projection_weight, w_gate, w_up, w_down, gain_attn, gain_mlp)
    cosine_table, sine_table = rope_tables(SEQUENCE_LENGTH, HEAD_SIZE)
    block = 16 * SEQUENCE_LENGTH
    count = tokens.shape[0] // block
    token_blocks = tokens.reshape(count, block, MODEL_WIDTH)
    cot_blocks = cotangent.reshape(count, block, MODEL_WIDTH)
    zeros = tuple((jnp.zeros(weight.shape, jnp.float32) for weight in weights))

    def step(carry, pair):
        piece, cot_piece = pair
        output, saved = layer_forward(piece, weights, cosine_table, sine_table)
        grad_piece, grads = layer_backward(cot_piece, saved, weights, cosine_table, sine_table)
        return (tuple((total + grad for total, grad in zip(carry, grads))), (output, grad_piece))
    totals, (outputs, grad_inputs) = lax.scan(step, zeros, (token_blocks, cot_blocks))
    return (outputs.reshape(-1, MODEL_WIDTH), grad_inputs.reshape(-1, MODEL_WIDTH), totals[0], totals[1], totals[2], totals[3], totals[4], totals[5], totals[6], totals[7], totals[8])
```

```python
import functools

import jax
import jax.numpy as jnp
import numpy as np
from jax import lax
from jax.experimental import pallas as pl
from jax.experimental.pallas import tpu as pltpu
from jax.sharding import PartitionSpec as P

QUERY_HEADS = 9
KEY_VALUE_HEADS = 3
HEAD_SIZE = 64
SEQUENCE_LENGTH = 192

EPS_NORM = 1e-05
ROPE_BASE = 100000.0


F32 = jnp.float32
BF16 = jnp.bfloat16
LANES = 128


def up_to(value, step):
    return -(-value // step) * step


def dot_nn(left, right):
    return lax.dot_general(left, right, (((1,), (0,)), ((), ())), preferred_element_type=F32)


def dot_nt(left, right):
    return lax.dot_general(left, right, (((1,), (1,)), ((), ())), preferred_element_type=F32)


def dot_tn(left, right):
    return lax.dot_general(left, right, (((0,), (0,)), ((), ())), preferred_element_type=F32)


def rope_tables():
    half = HEAD_SIZE // 2
    position = np.arange(SEQUENCE_LENGTH).astype(np.float32)
    freqs = np.power(
        np.float32(ROPE_BASE), -(np.arange(half).astype(np.float32) * np.float32(2.0 / HEAD_SIZE))
    ).astype(np.float32)
    angles = (position[:, None] * freqs[None, :]).astype(np.float32)
    cosine = np.cos(angles.astype(np.float64)).astype(np.float32)
    sine = np.sin(angles.astype(np.float64)).astype(np.float32)
    reps = LANES // HEAD_SIZE
    return (
        jnp.asarray(np.concatenate([cosine, cosine] * reps, 1)),
        jnp.asarray(np.concatenate([-sine, sine] * reps, 1)),
    )


def swap_halves(block):
    half = HEAD_SIZE // 2
    lane = lax.broadcasted_iota(jnp.int32, block.shape, block.ndim - 1)
    return jnp.where(
        lane % HEAD_SIZE < half,
        pltpu.roll(block, LANES - half, block.ndim - 1),
        pltpu.roll(block, half, block.ndim - 1),
    )


def lane_half(block, odd):
    lane = lax.broadcasted_iota(jnp.int32, block.shape, block.ndim - 1)
    keep = (lane >= HEAD_SIZE) if odd else (lane < HEAD_SIZE)
    return jnp.where(keep, block, jnp.zeros_like(block))


class Plan:
    def __init__(self, mesh, width, hidden):
        self.dp, self.fsdp = mesh.shape["dp"], mesh.shape["fsdp"]
        self.width, self.hidden = width, hidden
        self.kv = KEY_VALUE_HEADS * HEAD_SIZE
        self.lanes = up_to(width, LANES)
        self.nx, self.nc = self.dp // 2, 2
        self.nz, self.ny = self.fsdp // 2, 2
        s, d = self.fsdp, self.dp
        self.direct = (
            d % 2 == 0
            and s % 2 == 0
            and (width // s) % 8 == 0
            and (self.kv // s) % 8 == 0
            and ((width + self.kv) // s) % 16 == 0
            and (hidden // s // d) % 16 == 0
            and (hidden // d) % LANES == 0
        )
        if not self.direct:
            self.nx = self.nc = self.nz = self.ny = 1
        self.shards = self.nz * self.ny
        self.parts = self.nx * self.nc
        self.out_rows = width // self.shards
        self.kv_rows = self.kv // self.shards
        self.half_rows = self.out_rows + self.kv_rows
        self.ff_rows = hidden // self.shards // self.parts
        self.ff_cols = hidden // self.parts

    def key(self):
        return (self.dp, self.fsdp, self.width, self.hidden)


def attention_forward_kernel(plan, n_half, place, x_ref, cos_ref, sin_ref, *refs):
    pieces, refs = refs[: 2 * n_half], refs[2 * n_half :]
    (q_ref, k_ref, v_ref, attn_ref, prob_ref, wq_ref, wk_ref, wv_ref, wo_ref, gain_ref, pack, xs, sem) = refs
    width, lanes, kv = plan.width, plan.lanes, plan.kv
    x_at, c_at, z_at, y_at = place[0], place[1], place[2], place[3]
    copies = []
    count = 0
    for at, piece in enumerate(pieces):
        rc, ry = at // n_half, at % n_half
        half = (c_at + rc) % 2
        for k in range(plan.nz):
            shard = ((z_at - k + plan.nz) % plan.nz) * plan.ny + (y_at + ry) % plan.ny
            copies.append(pltpu.make_async_copy(piece.at[k], pack.at[half, shard], sem.at[count]))
            count += 1
    for copy in copies:
        copy.start()
    xs[:, lanes - LANES :] = jnp.zeros((xs.shape[0], LANES), F32)
    xs[:, :width] = x_ref[...].astype(F32)
    xfull = xs[...]
    inv = lax.rsqrt(jnp.sum(xfull * xfull, -1, keepdims=True) * (1.0 / width) + EPS_NORM)
    for copy in copies:
        copy.wait()
    rows, krows = plan.out_rows, plan.kv_rows
    qs, ks, vs, os = [], [], [], []
    for s in range(plan.shards):
        first = pack[0, s].astype(F32)
        second = pack[1, s].astype(F32)
        qs.append(first[:rows])
        ks.append(first[rows:])
        vs.append(second[:krows])
        os.append(second[krows:])
    tail = jnp.zeros((lanes - width, lanes), F32)
    wq_full = jnp.concatenate(qs + [tail], 0)
    lane = lax.broadcasted_iota(jnp.int32, (lanes, lanes), 1)
    wq_ref[...] = jnp.where(lane < width, wq_full, 0.0).astype(BF16)
    kv_pad = 2 * LANES
    ktail = jnp.zeros((kv_pad - kv, lanes), F32)
    wk_ref[...] = jnp.concatenate(ks + [ktail], 0).astype(BF16)
    wv_ref[...] = jnp.concatenate(vs + [ktail], 0).astype(BF16)
    wo_ref[...] = jnp.concatenate(os + [tail], 0).astype(BF16)
    turned = wq_full[:, lanes - LANES :].T
    at = width - (lanes - LANES)
    gain_ref[...] = turned[at : at + 8]
    gain = turned[at : at + 1]
    normed = (xfull * inv * gain).astype(BF16)
    tokens = xs.shape[0]
    n_seq = tokens // SEQUENCE_LENGTH
    cos = cos_ref[...][None]
    sin = sin_ref[...][None]

    def rotate(block):
        cube = block.reshape(n_seq, SEQUENCE_LENGTH, LANES)
        return (cube * cos + swap_halves(cube) * sin).reshape(tokens, LANES)

    q = dot_nt(normed, wq_ref[...])
    for b in range(lanes // LANES):
        q_ref[:, b * LANES : (b + 1) * LANES] = rotate(q[:, b * LANES : (b + 1) * LANES]).astype(BF16)
    k = dot_nt(normed, wk_ref[...])
    v = dot_nt(normed, wv_ref[...])
    for b in range(2):
        kb = rotate(k[:, b * LANES : (b + 1) * LANES])
        vb = v[:, b * LANES : (b + 1) * LANES]
        k_ref[:, b * LANES : (b + 1) * LANES] = kb.astype(BF16)
        v_ref[:, b * LANES : (b + 1) * LANES] = vb.astype(BF16)
        k_ref[:, (b + 2) * LANES : (b + 3) * LANES] = pltpu.roll(kb, HEAD_SIZE, 1).astype(BF16)
        v_ref[:, (b + 2) * LANES : (b + 3) * LANES] = pltpu.roll(vb, HEAD_SIZE, 1).astype(BF16)

    shape = (SEQUENCE_LENGTH, SEQUENCE_LENGTH)
    allowed = lax.broadcasted_iota(jnp.int32, shape, 0) >= lax.broadcasted_iota(jnp.int32, shape, 1)

    def one_sequence(n, carry):
        at_rows = pl.ds(pl.multiple_of(n * SEQUENCE_LENGTH, SEQUENCE_LENGTH), SEQUENCE_LENGTH)
        for pair in range(lanes // LANES):
            q2 = q_ref[at_rows, pair * LANES : (pair + 1) * LANES]
            total = None
            for odd in range(2):
                h = pair * 2 + odd
                if h >= QUERY_HEADS:
                    continue
                kf = head_form(k_ref, at_rows, h)
                vf = head_form(v_ref, at_rows, h)
                scores = dot_nt(q2, kf) * HEAD_SIZE ** (-0.5)
                expo = jnp.where(allowed, jnp.exp(jnp.where(allowed, scores, 0.0)), 0.0)
                p = (expo * (1.0 / jnp.sum(expo, -1, keepdims=True))).astype(BF16)
                prob_ref[n, h] = p
                part = dot_nn(p, vf)
                total = part if total is None else total + part
            attn_ref[at_rows, pair * LANES : (pair + 1) * LANES] = total.astype(BF16)
        return carry

    lax.fori_loop(0, n_seq, one_sequence, 0)


def head_form(ref, at_rows, h):
    group, odd = h // (QUERY_HEADS // KEY_VALUE_HEADS), h % 2
    block = group // 2 + (2 if group % 2 != odd else 0)
    return lane_half(ref[at_rows, block * LANES : (block + 1) * LANES], odd)


def mlp_kernel(plan, chunks, n_ff, n_down, place, x_ref, dy_ref, attn_ref, wo_ref, gain_ref, *refs):
    gates, refs = refs[:n_ff], refs[n_ff:]
    ups, refs = refs[:n_ff], refs[n_ff:]
    downs, refs = refs[:n_down], refs[n_down:]
    out_ref, dmid_ref, dgain_ref, refs = refs[0], refs[1], refs[2], refs[3:]
    gg_out, refs = refs[: plan.nc], refs[plan.nc :]
    gu_out, refs = refs[: plan.nc], refs[plan.nc :]
    gd_out, refs = refs[: plan.nc], refs[plan.nc :]
    (wg, wu, wd3, wd, gg, gu, gd, xs, sem) = refs
    width, lanes, hidden = plan.width, plan.lanes, plan.hidden
    x_at, c_at, z_at, y_at = place[0], place[1], place[2], place[3]
    rows, cols = plan.ff_rows, plan.ff_cols
    loads = []
    count = 0

    def source(rc, rx, ry, rz, sign):
        shard = ((z_at + sign * rz + plan.nz) % plan.nz) * plan.ny + (y_at + ry) % plan.ny
        part = ((x_at + rx) % plan.nx) * plan.nc + (c_at + rc) % plan.nc
        return shard, part

    order = [(rc, rx, ry) for rc in range(plan.nc) for rx in range(plan.nx) for ry in range(plan.ny)]
    for operands, dest in ((gates, wg), (ups, wu)):
        for (rc, rx, ry), piece in zip(order, operands):
            for k in range(plan.nz):
                shard, part = source(rc, rx, ry, k, -1)
                at = pl.multiple_of((shard * plan.parts + part) * rows, rows)
                loads.append(pltpu.make_async_copy(piece.at[k], dest.at[pl.ds(at, rows)], sem.at[count]))
                count += 1
    for (rc, rx, ry), piece in zip(order, downs):
        for k in range(plan.nz):
            shard, part = source(rc, rx, ry, k, -1)
            at = pl.multiple_of(part * cols, cols)
            loads.append(
                pltpu.make_async_copy(piece.at[k], wd3.at[shard, :, pl.ds(at, cols)], sem.at[count])
            )
            count += 1
    for copy in loads:
        copy.start()
    tokens = xs.shape[0]
    xs[:, lanes - LANES :] = jnp.zeros((tokens, LANES), F32)
    xs[:, :width] = x_ref[...].astype(F32)
    mid = xs[...] + dot_nt(attn_ref[...], wo_ref[...])
    inv = lax.rsqrt(jnp.sum(mid * mid, -1, keepdims=True) * (1.0 / width) + EPS_NORM)
    gain = gain_ref[1:2]
    unit = mid * inv
    normed = (unit * gain).astype(BF16)
    xs[:, :width] = dy_ref[...].astype(F32)
    dy = xs[...].astype(BF16)
    for copy in loads:
        copy.wait()
    wd[width:, :] = jnp.zeros((lanes - width, hidden), BF16)
    wd[:width, :] = jnp.concatenate([wd3[s].astype(F32) for s in range(plan.shards)], 0).astype(BF16)
    step = hidden // chunks
    out = mid
    dnormed = jnp.zeros((tokens, lanes), F32)
    for j in range(chunks):
        at = slice(j * step, (j + 1) * step)
        gate = dot_nt(normed, wg[at, :])
        upper = dot_nt(normed, wu[at, :])
        dhidden = dot_nn(dy, wd[:, at])
        sigma = 1.0 / (1.0 + jnp.exp(-gate))
        act = gate * sigma
        hid = (act * upper).astype(BF16)
        out = out + dot_nt(hid, wd[:, at])
        dgate = (dhidden * upper * sigma * (1.0 + gate * (1.0 - sigma))).astype(BF16)
        dupper = (dhidden * act).astype(BF16)
        dnormed = dnormed + dot_nn(dgate, wg[at, :]) + dot_nn(dupper, wu[at, :])
        gg[at, :] = dot_tn(dgate, normed).astype(BF16)
        gu[at, :] = dot_tn(dupper, normed).astype(BF16)
        down = dot_tn(dy, hid)
        for s in range(plan.shards):
            gd[s, :, at] = down[s * plan.out_rows : (s + 1) * plan.out_rows].astype(BF16)
    stores = []
    count = 0
    for rc in range(plan.nc):
        for rx in range(plan.nx):
            for ry in range(plan.ny):
                for rz in range(plan.nz):
                    shard, part = source(rc, rx, ry, rz, 1)
                    at = pl.multiple_of((shard * plan.parts + part) * rows, rows)
                    col = pl.multiple_of(part * cols, cols)
                    stores.append(
                        pltpu.make_async_copy(gg.at[pl.ds(at, rows)], gg_out[rc].at[rx, ry, rz], sem.at[count])
                    )
                    stores.append(
                        pltpu.make_async_copy(gu.at[pl.ds(at, rows)], gu_out[rc].at[rx, ry, rz], sem.at[count + 1])
                    )
                    stores.append(
                        pltpu.make_async_copy(
                            gd.at[shard, :, pl.ds(col, cols)], gd_out[rc].at[rx, ry, rz], sem.at[count + 2]
                        )
                    )
                    count += 3
    for copy in stores:
        copy.start()
    out_ref[...] = out[:, :width].astype(BF16)
    total = jnp.sum(dnormed * unit, 0, keepdims=True)
    dgain_ref[...] = jnp.broadcast_to(total, dgain_ref.shape)
    scaled = dnormed * gain
    dmid_ref[...] = inv * (scaled - unit * (jnp.sum(scaled * unit, -1, keepdims=True) * (1.0 / width))) + xs[...]
    for copy in stores:
        copy.wait()


def attention_backward_kernel(plan, place, x_ref, dmid_ref, dgain_ref, attn_ref, q_ref, k_ref, v_ref, prob_ref,
                              wq_ref, wk_ref, wv_ref, wo_ref, gain_ref, cos_ref, sin_ref, *refs):
    dx_ref, refs = refs[0], refs[1:]
    packs, refs = refs[: plan.nc], refs[plan.nc :]
    (da, dq, dkv, pack, xs, sem) = refs
    width, lanes, kv = plan.width, plan.lanes, plan.kv
    x_at, c_at, z_at, y_at = place[0], place[1], place[2], place[3]
    tokens = xs.shape[0]
    n_seq = tokens // SEQUENCE_LENGTH
    xs[:, lanes - LANES :] = jnp.zeros((tokens, LANES), F32)
    xs[:, :width] = x_ref[...].astype(F32)
    dmid_b = dmid_ref[...].astype(BF16)
    grad_out = dot_tn(dmid_b, attn_ref[...])
    da[...] = dot_nn(dmid_b, wo_ref[...]).astype(BF16)
    cos = cos_ref[...]
    sin = sin_ref[...]
    kv_pad = 2 * LANES

    def unrotate(block):
        return block * cos - swap_halves(block) * sin

    def one_sequence(n, carry):
        at_rows = pl.ds(pl.multiple_of(n * SEQUENCE_LENGTH, SEQUENCE_LENGTH), SEQUENCE_LENGTH)
        dk = [None] * KEY_VALUE_HEADS
        dv = [None] * KEY_VALUE_HEADS
        for pair in range(lanes // LANES):
            lanes_at = slice(pair * LANES, (pair + 1) * LANES)
            q2 = q_ref[at_rows, lanes_at]
            da2 = da[at_rows, lanes_at]
            prod = da2.astype(F32) * attn_ref[at_rows, lanes_at].astype(F32)
            total = None
            for odd in range(2):
                h = pair * 2 + odd
                if h >= QUERY_HEADS:
                    continue
                group = h // (QUERY_HEADS // KEY_VALUE_HEADS)
                kf = head_form(k_ref, at_rows, h)
                vf = head_form(v_ref, at_rows, h)
                p = prob_ref[n, h]
                delta = jnp.sum(lane_half(prod, odd), -1, keepdims=True)
                dp = dot_nt(da2, vf)
                ds = (p.astype(F32) * (dp - delta) * HEAD_SIZE ** (-0.5)).astype(BF16)
                part = dot_nn(ds, kf)
                total = part if total is None else total + part
                dvp = dot_tn(p, lane_half(da2, odd))
                dkp = dot_tn(ds, lane_half(q2, odd))
                dv[group] = dvp if dv[group] is None else dv[group] + dvp
                dk[group] = dkp if dk[group] is None else dk[group] + dkp
            dq[at_rows, lanes_at] = unrotate(total).astype(BF16)
        for slot, (parts, turn) in enumerate(((dk, unrotate), (dv, lambda b: b))):
            whole = [g + pltpu.roll(g, HEAD_SIZE, 1) for g in parts]
            for b in range(2):
                block = lane_half(whole[2 * b], 0)
                if 2 * b + 1 < KEY_VALUE_HEADS:
                    block = block + lane_half(whole[2 * b + 1], 1)
                dkv[slot, at_rows, b * LANES : (b + 1) * LANES] = turn(block).astype(BF16)
        return carry

    lax.fori_loop(0, n_seq, one_sequence, 0)
    xfull = xs[...]
    inv = lax.rsqrt(jnp.sum(xfull * xfull, -1, keepdims=True) * (1.0 / width) + EPS_NORM)
    gain = gain_ref[0:1]
    unit = xfull * inv
    normed = (unit * gain).astype(BF16)
    dnormed = dot_nn(dq[...], wq_ref[...]) + dot_nn(dkv[0], wk_ref[...]) + dot_nn(dkv[1], wv_ref[...])
    lane = lax.broadcasted_iota(jnp.int32, (1, lanes), 1)
    dnormed = jnp.where(lane < width, dnormed, 0.0)
    dgain = jnp.sum(dnormed * unit, 0, keepdims=True)
    grad_q = dot_tn(dq[...], normed)
    grad_k = dot_tn(dkv[0], normed)
    grad_v = dot_tn(dkv[1], normed)
    at = width - (lanes - LANES)
    row = lax.broadcasted_iota(jnp.int32, (LANES, lanes), 0)
    sheet = jnp.where(row == at, dgain, 0.0) + jnp.where(row == at + 1, dgain_ref[0:1], 0.0)
    side = sheet.T
    grad_q = jnp.concatenate([grad_q[:, : lanes - LANES], grad_q[:, lanes - LANES :] + side], 1)
    rows, krows = plan.out_rows, plan.kv_rows
    for s in range(plan.shards):
        a, b = slice(s * rows, (s + 1) * rows), slice(s * krows, (s + 1) * krows)
        pack[0, s] = jnp.concatenate([grad_q[a], grad_k[b]], 0).astype(BF16)
        pack[1, s] = jnp.concatenate([grad_v[b], grad_out[a]], 0).astype(BF16)
    stores = []
    count = 0
    for rc in range(2):
        for ry in range(plan.ny):
            for rz in range(plan.nz):
                shard = ((z_at + rz) % plan.nz) * plan.ny + (y_at + ry) % plan.ny
                half = (c_at + rc) % 2
                target = packs[rc] if plan.nc == 2 else packs[0].at[rc]
                stores.append(pltpu.make_async_copy(pack.at[half, shard], target.at[ry, rz], sem.at[count]))
                count += 1
    for copy in stores:
        copy.start()
    scaled = dnormed * gain
    dx = inv * (scaled - unit * (jnp.sum(scaled * unit, -1, keepdims=True) * (1.0 / width))) + dmid_ref[...]
    dx_ref[...] = dx[:, :width].astype(BF16)
    for copy in stores:
        copy.wait()


VMEM = pl.BlockSpec(memory_space=pltpu.VMEM)
SMEM = pl.BlockSpec(memory_space=pltpu.SMEM)
ANY = pl.BlockSpec(memory_space=pl.ANY)


def shape_of(dims, kind):
    return jax.ShapeDtypeStruct(dims, kind)


def attention_forward(plan, place, tokens, cos, sin, pieces):
    rows, lanes = tokens.shape[0], plan.lanes
    n_seq = rows // SEQUENCE_LENGTH
    return pl.pallas_call(
        functools.partial(attention_forward_kernel, plan, len(pieces) // 2),
        name="attention_forward",
        in_specs=[SMEM, VMEM, VMEM, VMEM] + [ANY] * len(pieces),
        out_specs=[VMEM] * 10,
        out_shape=[
            shape_of((rows, lanes), BF16),
            shape_of((rows, 4 * LANES), BF16),
            shape_of((rows, 4 * LANES), BF16),
            shape_of((rows, lanes), BF16),
            shape_of((n_seq, QUERY_HEADS, SEQUENCE_LENGTH, SEQUENCE_LENGTH), BF16),
            shape_of((lanes, lanes), BF16),
            shape_of((2 * LANES, lanes), BF16),
            shape_of((2 * LANES, lanes), BF16),
            shape_of((lanes, lanes), BF16),
            shape_of((8, lanes), F32),
        ],
        scratch_shapes=[
            pltpu.VMEM((2, plan.shards, plan.half_rows, lanes), BF16),
            pltpu.VMEM((rows, lanes), F32),
            pltpu.SemaphoreType.DMA((len(pieces) * plan.nz,)),
        ],
    )(place, tokens, cos, sin, *pieces)


def mlp(plan, place, tokens, cotangent, attn, wo, gain, gates, ups, downs):
    rows, lanes = tokens.shape[0], plan.lanes
    ff = shape_of((plan.nx, plan.ny, plan.nz, plan.ff_rows, lanes), BF16)
    dn = shape_of((plan.nx, plan.ny, plan.nz, plan.out_rows, plan.ff_cols), BF16)
    n_out = 3 * plan.nc
    return pl.pallas_call(
        functools.partial(mlp_kernel, plan, 2, len(gates), len(downs)),
        name="mlp",
        in_specs=[SMEM] + [VMEM] * 5 + [ANY] * (len(gates) + len(ups) + len(downs)),
        out_specs=[VMEM] * 3 + [ANY] * n_out,
        out_shape=[
            shape_of((rows, plan.width), BF16),
            shape_of((rows, lanes), F32),
            shape_of((8, lanes), F32),
        ]
        + [ff] * (2 * plan.nc)
        + [dn] * plan.nc,
        scratch_shapes=[
            pltpu.VMEM((plan.hidden, lanes), BF16),
            pltpu.VMEM((plan.hidden, lanes), BF16),
            pltpu.VMEM((plan.shards, plan.out_rows, plan.hidden), BF16),
            pltpu.VMEM((lanes, plan.hidden), BF16),
            pltpu.VMEM((plan.hidden, lanes), BF16),
            pltpu.VMEM((plan.hidden, lanes), BF16),
            pltpu.VMEM((plan.shards, plan.out_rows, plan.hidden), BF16),
            pltpu.VMEM((rows, lanes), F32),
            pltpu.SemaphoreType.DMA((3 * plan.shards * plan.parts,)),
        ],
    )(place, tokens, cotangent, attn, wo, gain, *gates, *ups, *downs)


def attention_backward(plan, place, tokens, dmid, dgain, attn, q, k, v, prob, wq, wk, wv, wo, gain, cos, sin):
    rows, lanes = tokens.shape[0], plan.lanes
    block = (plan.ny, plan.nz, plan.half_rows, lanes)
    if plan.nc == 2:
        packs = [shape_of(block, BF16)] * 2
    else:
        packs = [shape_of((2,) + block, BF16)]
    return pl.pallas_call(
        functools.partial(attention_backward_kernel, plan),
        name="attention_backward",
        in_specs=[SMEM] + [VMEM] * 15,
        out_specs=[VMEM] + [ANY] * len(packs),
        out_shape=[shape_of((rows, plan.width), BF16)] + packs,
        scratch_shapes=[
            pltpu.VMEM((rows, lanes), BF16),
            pltpu.VMEM((rows, lanes), BF16),
            pltpu.VMEM((2, rows, 2 * LANES), BF16),
            pltpu.VMEM((2, plan.shards, plan.half_rows, lanes), BF16),
            pltpu.VMEM((rows, lanes), F32),
            pltpu.SemaphoreType.DMA((2 * plan.shards,)),
        ],
    )(place, tokens, dmid, dgain, attn, q, k, v, prob, wq, wk, wv, wo, gain, cos, sin)


def shift(plan, dim, amount):
    if dim in "xc":
        axis, outer, inner, first = "dp", plan.nx, plan.nc, dim == "x"
    else:
        axis, outer, inner, first = "fsdp", plan.nz, plan.ny, dim == "z"
    pairs = []
    for o in range(outer):
        for i in range(inner):
            to = ((o + amount) % outer, i) if first else (o, (i + amount) % inner)
            pairs.append((o * inner + i, to[0] * inner + to[1]))
    return axis, pairs


def send(plan, value, dim, amount=1):
    axis, pairs = shift(plan, dim, amount)
    return lax.ppermute(value, axis, pairs)


def spread(plan, piece, dims):
    stack = jnp.stack([piece] + [send(plan, piece, "z", k) for k in range(1, plan.nz)])
    held = {(0, 0, 0): stack}
    for dim in dims:
        at = "cxy".index(dim)
        for place, value in list(held.items()):
            place = list(place)
            place[at] = 1
            held[tuple(place)] = send(plan, value, dim)
    return held


def add(a, b):
    return (a.astype(F32) + b.astype(F32)).astype(BF16)


def gather_z(plan, stack):
    total = stack[0].astype(F32)
    for k in range(1, plan.nz):
        total = total + send(plan, stack[k], "z", k).astype(F32)
    return total.astype(BF16)


def body(plan, tokens, cotangent, w_query, w_key, w_value, w_out, w_gate, w_up, w_down, gain_attn, gain_mlp):
    cos, sin = rope_tables()
    width, lanes, hidden = plan.width, plan.lanes, plan.hidden
    d_at, s_at = lax.axis_index("dp"), lax.axis_index("fsdp")
    if plan.direct:
        place = jnp.stack([d_at // plan.nc, d_at % plan.nc, s_at // plan.ny, s_at % plan.ny]).astype(jnp.int32)
    else:
        place = jnp.zeros((4,), jnp.int32)

    def widen(rows, extra=None):
        rest = lanes - width
        if extra is None:
            return jnp.pad(rows, ((0, 0), (0, rest)))
        side = jnp.pad(extra, ((0, rows.shape[0] - extra.shape[0]), (0, rest - extra.shape[1])))
        return jnp.concatenate([rows, side], 1)

    def all_rows(w):
        return lax.all_gather(w.T, "fsdp", axis=0, tiled=True)

    if plan.direct:
        gains = jnp.stack([gain_attn, gain_mlp], 1)
        first = widen(jnp.concatenate([w_query.T, w_key.T], 0), gains)
        second = widen(jnp.concatenate([w_value.T, w_out.T], 0))
        own = jnp.where(d_at % plan.nc == 0, first, second)
        gate_own = widen(lax.dynamic_slice_in_dim(w_gate, d_at * plan.ff_rows, plan.ff_rows, 1).T)
        up_own = widen(lax.dynamic_slice_in_dim(w_up, d_at * plan.ff_rows, plan.ff_rows, 1).T)
        down_own = lax.dynamic_slice_in_dim(w_down, d_at * plan.ff_cols, plan.ff_cols, 0).T
        held = spread(plan, own, "yc")
        pieces = [held[rc, 0, ry] for rc in range(2) for ry in range(2)]
        keys = [(rc, rx, ry) for rc in range(plan.nc) for rx in range(plan.nx) for ry in range(plan.ny)]
        held = spread(plan, gate_own, "yxc")
        gates = [held[key] for key in keys]
        held = spread(plan, up_own, "yxc")
        ups = [held[key] for key in keys]
        held = spread(plan, down_own, "xyc")
        downs = [held[key] for key in keys]
    else:
        gains = jnp.stack(
            [lax.all_gather(g, "fsdp", axis=0, tiled=True) for g in (gain_attn, gain_mlp)], 1
        )
        pieces = [
            widen(jnp.concatenate([all_rows(w_query), all_rows(w_key)], 0), gains)[None],
            widen(jnp.concatenate([all_rows(w_value), all_rows(w_out)], 0))[None],
        ]
        gates = [widen(all_rows(w_gate))[None]]
        ups = [widen(all_rows(w_up))[None]]
        downs = [all_rows(w_down)[None]]

    q, k, v, attn, prob, wq, wk, wv, wo, gain = attention_forward(plan, place, tokens, cos, sin, pieces)
    output, dmid, dgain, *grads = mlp(plan, place, tokens, cotangent, attn, wo, gain, gates, ups, downs)
    grad_tokens, *packs = attention_backward(
        plan, place, tokens, dmid, dgain, attn, q, k, v, prob, wq, wk, wv, wo, gain, cos, sin
    )
    rows, krows = plan.out_rows, plan.kv_rows

    if plan.direct:

        def fold(keep, away, dims):
            got = send(plan, away, "c")
            take = {"x": lambda t, i: t[i], "y": lambda t, i: t[:, i]}[dims[0]]
            there = send(plan, add(take(keep, 1), take(got, 1)), dims[0])
            part = add(add(take(keep, 0), take(got, 0)), there)
            part = add(part[0], send(plan, part[1], dims[1]))
            part = gather_z(plan, part)
            both = jnp.stack([part, send(plan, part, "x")])
            other = send(plan, both, "c")
            quads = jnp.stack([both, other], 1)
            x_at, c_at = d_at // plan.nc, d_at % plan.nc
            quads = jnp.where(c_at == 0, quads, quads[:, ::-1])
            return jnp.where(x_at == 0, quads, quads[::-1])

        def ff(quads):
            return quads.reshape(plan.parts * plan.ff_rows, lanes)[:, :width].astype(F32).T

        n = plan.nc
        grad_gate = ff(fold(grads[0], grads[1], "xy"))
        grad_up = ff(fold(grads[n], grads[n + 1], "xy"))
        quads = fold(grads[2 * n], grads[2 * n + 1], "yx")
        grad_down = quads.transpose(0, 1, 3, 2).reshape(hidden, rows).astype(F32)
        part = add(packs[0], send(plan, packs[1], "c"))
        part = add(part[0], send(plan, part[1], "y"))
        part = gather_z(plan, part)
        part = add(part, send(plan, part, "x"))
        other = send(plan, part, "c")
        c_at = d_at % plan.nc
        one = jnp.where(c_at == 0, part, other).astype(F32)
        two = jnp.where(c_at == 0, other, part).astype(F32)
    else:

        def total(value):
            part = lax.psum_scatter(value.astype(F32), "fsdp", scatter_dimension=0, tiled=True)
            return lax.psum(part, "dp")

        grad_gate = total(grads[0].reshape(hidden, lanes)[:, :width]).T
        grad_up = total(grads[1].reshape(hidden, lanes)[:, :width]).T
        grad_down = total(grads[2].reshape(width, hidden)).T
        whole = packs[0].reshape(2, width + plan.kv, lanes)
        one = jnp.concatenate([total(whole[0, :width]), total(whole[0, width:])], 0)
        two = jnp.concatenate([total(whole[1, : plan.kv]), total(whole[1, plan.kv :])], 0)
        rows, krows = width // plan.fsdp, plan.kv // plan.fsdp
    return (
        output,
        grad_tokens,
        one[:rows, :width].T,
        one[rows:, :width].T,
        two[:krows, :width].T,
        two[krows:, :width].T,
        grad_gate,
        grad_up,
        grad_down,
        one[:rows, width],
        one[:rows, width + 1],
    )


def solution(mesh):
    rows = P(("dp", "fsdp"), None)
    cols = P(None, "fsdp")
    one = P("fsdp")

    def run(*args):
        plan = Plan(mesh, args[0].shape[1], args[8].shape[0])
        return jax.shard_map(
            functools.partial(body, plan),
            mesh=mesh,
            in_specs=(rows, rows) + (cols,) * 7 + (one, one),
            out_specs=(rows, rows) + (cols,) * 7 + (one, one),
            check_vma=False,
        )(*args)

    return run
```

```python
import functools

import jax
import jax.numpy as jnp
import numpy as np
from jax import lax
from jax.experimental import pallas as pl
from jax.experimental.pallas import tpu as pltpu
from jax.sharding import PartitionSpec as P


QUERY_HEADS = 9
KEY_VALUE_HEADS = 3
HEAD_SIZE = 64
SEQUENCE_LENGTH = 192

EPS_NORM = 1e-05
ROPE_BASE = 100000.0


F32 = jnp.float32
BF16 = jnp.bfloat16
LANES = 128


def up_to(value, step):
    return -(-value // step) * step


def dot_nn(left, right):
    return lax.dot_general(left, right, (((1,), (0,)), ((), ())), preferred_element_type=F32)


def dot_nt(left, right):
    return lax.dot_general(left, right, (((1,), (1,)), ((), ())), preferred_element_type=F32)


def dot_tn(left, right):
    return lax.dot_general(left, right, (((0,), (0,)), ((), ())), preferred_element_type=F32)


def rope_tables():
    half = HEAD_SIZE // 2
    position = np.arange(SEQUENCE_LENGTH).astype(np.float32)
    freqs = np.power(
        np.float32(ROPE_BASE), -(np.arange(half).astype(np.float32) * np.float32(2.0 / HEAD_SIZE))
    ).astype(np.float32)
    angles = (position[:, None] * freqs[None, :]).astype(np.float32)
    cosine = np.cos(angles.astype(np.float64)).astype(np.float32)
    sine = np.sin(angles.astype(np.float64)).astype(np.float32)
    reps = LANES // HEAD_SIZE
    return (
        jnp.asarray(np.concatenate([cosine, cosine] * reps, 1)),
        jnp.asarray(np.concatenate([-sine, sine] * reps, 1)),
    )


def swap_halves(block):
    half = HEAD_SIZE // 2
    lane = lax.broadcasted_iota(jnp.int32, block.shape, block.ndim - 1)
    return jnp.where(
        lane % HEAD_SIZE < half,
        pltpu.roll(block, LANES - half, block.ndim - 1),
        pltpu.roll(block, half, block.ndim - 1),
    )


def lane_half(block, odd):
    lane = lax.broadcasted_iota(jnp.int32, block.shape, block.ndim - 1)
    keep = (lane >= HEAD_SIZE) if odd else (lane < HEAD_SIZE)
    return jnp.where(keep, block, jnp.zeros_like(block))


class Plan:
    def __init__(self, mesh, width, hidden):
        self.dp, self.fsdp = mesh.shape["dp"], mesh.shape["fsdp"]
        self.width, self.hidden = width, hidden
        self.kv = KEY_VALUE_HEADS * HEAD_SIZE
        self.lanes = up_to(width, LANES)
        self.nx, self.nc = self.dp // 2, 2
        self.nz, self.ny = self.fsdp // 2, 2
        s, d = self.fsdp, self.dp
        self.direct = (
            d % 2 == 0
            and s % 2 == 0
            and (s // 2) & (s // 2 - 1) == 0
            and (width // s) % 8 == 0
            and (self.kv // s) % 8 == 0
            and ((width + self.kv) // s) % (16 * (d // 2)) == 0
            and (hidden // s // d) % 16 == 0
            and (hidden // d) % LANES == 0
        )
        if not self.direct:
            self.nx = self.nc = self.nz = self.ny = 1
        self.shards = self.nz * self.ny
        self.parts = self.nx * self.nc
        self.out_rows = width // self.shards
        self.kv_rows = self.kv // self.shards
        self.half_rows = self.out_rows + self.kv_rows
        self.ff_rows = hidden // self.shards // self.parts
        self.ff_cols = hidden // self.parts

    def key(self):
        return (self.dp, self.fsdp, self.width, self.hidden)


def attention_forward_kernel(plan, n_half, place, x_ref, cos_ref, sin_ref, *refs):
    pieces, refs = refs[: 2 * n_half], refs[2 * n_half :]
    (q_ref, k_ref, v_ref, attn_ref, prob_ref, wq_ref, wk_ref, wv_ref, wo_ref, gain_ref, pack, xs, sem) = refs
    width, lanes, kv = plan.width, plan.lanes, plan.kv
    c_at, z_at, y_at = place[1], place[2], place[3]
    copies = []
    count = 0
    for at, piece in enumerate(pieces):
        rc, ry = at // n_half, at % n_half
        half = (c_at + rc) % 2
        for k in range(plan.nz):
            shard = (z_at ^ k) * plan.ny + (y_at + ry) % plan.ny
            copies.append(pltpu.make_async_copy(piece.at[k], pack.at[half, shard], sem.at[count]))
            count += 1
    for copy in copies:
        copy.start()
    xs[:, lanes - LANES :] = jnp.zeros((xs.shape[0], LANES), F32)
    xs[:, :width] = x_ref[...].astype(F32)
    xfull = xs[...]
    inv = lax.rsqrt(jnp.sum(xfull * xfull, -1, keepdims=True) * (1.0 / width) + EPS_NORM)
    for copy in copies:
        copy.wait()
    rows, krows = plan.out_rows, plan.kv_rows
    qs, ks, vs, os = [], [], [], []
    for s in range(plan.shards):
        first = pack[0, s].astype(F32)
        second = pack[1, s].astype(F32)
        qs.append(first[:rows])
        ks.append(first[rows:])
        vs.append(second[:krows])
        os.append(second[krows:])
    tail = jnp.zeros((lanes - width, lanes), F32)
    wq_full = jnp.concatenate(qs + [tail], 0)
    lane = lax.broadcasted_iota(jnp.int32, (lanes, lanes), 1)
    wq_ref[...] = jnp.where(lane < width, wq_full, 0.0).astype(BF16)
    kv_pad = 2 * LANES
    ktail = jnp.zeros((kv_pad - kv, lanes), F32)
    wk_ref[...] = jnp.concatenate(ks + [ktail], 0).astype(BF16)
    wv_ref[...] = jnp.concatenate(vs + [ktail], 0).astype(BF16)
    wo_ref[...] = jnp.concatenate(os + [tail], 0).astype(BF16)
    turned = wq_full[:, lanes - LANES :].T
    at = width - (lanes - LANES)
    gain_ref[...] = turned[at : at + 8]
    gain = turned[at : at + 1]
    normed = (xfull * inv * gain).astype(BF16)
    tokens = xs.shape[0]
    n_seq = tokens // SEQUENCE_LENGTH
    cos = cos_ref[...][None]
    sin = sin_ref[...][None]

    def rotate(block):
        cube = block.reshape(n_seq, SEQUENCE_LENGTH, LANES)
        return (cube * cos + swap_halves(cube) * sin).reshape(tokens, LANES)

    q = dot_nt(normed, wq_ref[...])
    for b in range(lanes // LANES):
        q_ref[:, b * LANES : (b + 1) * LANES] = rotate(q[:, b * LANES : (b + 1) * LANES]).astype(BF16)
    k = dot_nt(normed, wk_ref[...])
    v = dot_nt(normed, wv_ref[...])
    for b in range(2):
        kb = rotate(k[:, b * LANES : (b + 1) * LANES])
        vb = v[:, b * LANES : (b + 1) * LANES]
        k_ref[:, b * LANES : (b + 1) * LANES] = kb.astype(BF16)
        v_ref[:, b * LANES : (b + 1) * LANES] = vb.astype(BF16)
        k_ref[:, (b + 2) * LANES : (b + 3) * LANES] = pltpu.roll(kb, HEAD_SIZE, 1).astype(BF16)
        v_ref[:, (b + 2) * LANES : (b + 3) * LANES] = pltpu.roll(vb, HEAD_SIZE, 1).astype(BF16)

    shape = (SEQUENCE_LENGTH, SEQUENCE_LENGTH)
    allowed = lax.broadcasted_iota(jnp.int32, shape, 0) >= lax.broadcasted_iota(jnp.int32, shape, 1)

    def one_sequence(n, carry):
        at_rows = pl.ds(pl.multiple_of(n * SEQUENCE_LENGTH, SEQUENCE_LENGTH), SEQUENCE_LENGTH)
        for pair in range(lanes // LANES):
            q2 = q_ref[at_rows, pair * LANES : (pair + 1) * LANES]
            total = None
            for odd in range(2):
                h = pair * 2 + odd
                if h >= QUERY_HEADS:
                    continue
                kf = head_form(k_ref, at_rows, h)
                vf = head_form(v_ref, at_rows, h)
                scores = dot_nt(q2, kf) * HEAD_SIZE ** (-0.5)
                expo = jnp.where(allowed, jnp.exp(jnp.where(allowed, scores, 0.0)), 0.0)
                p = (expo * (1.0 / jnp.sum(expo, -1, keepdims=True))).astype(BF16)
                prob_ref[n, h] = p
                part = dot_nn(p, vf)
                total = part if total is None else total + part
            attn_ref[at_rows, pair * LANES : (pair + 1) * LANES] = total.astype(BF16)
        return carry

    lax.fori_loop(0, n_seq, one_sequence, 0)


def head_form(ref, at_rows, h):
    group, odd = h // (QUERY_HEADS // KEY_VALUE_HEADS), h % 2
    block = group // 2 + (2 if group % 2 != odd else 0)
    return lane_half(ref[at_rows, block * LANES : (block + 1) * LANES], odd)


def mlp_kernel(plan, first, last, place, dy_ref, gain_ref, *refs):
    if first:
        x_ref, attn_ref, wo_ref, refs = refs[0], refs[1], refs[2], refs[3:]
    else:
        mid_in, out_in, dn_in, refs = refs[0], refs[1], refs[2], refs[3:]
    n_pieces = plan.nc * plan.ny
    gates, refs = refs[:n_pieces], refs[n_pieces:]
    downs, refs = refs[:n_pieces], refs[n_pieces:]
    if last:
        out_ref, dmid_ref, dgain_ref, refs = refs[0], refs[1], refs[2], refs[3:]
    else:
        mid_ref, out_ref, dn_ref, refs = refs[0], refs[1], refs[2], refs[3:]
    gg_out, refs = refs[: plan.nc], refs[plan.nc :]
    gd_out, refs = refs[: plan.nc], refs[plan.nc :]
    (wg, wu, wd3, wd, gg, gu, gd, xs, sem) = refs
    width, lanes = plan.width, plan.lanes
    z_at, y_at = place[2], place[3]
    rows, cols = plan.ff_rows, plan.ff_cols
    loads, late = [], []
    count = 0
    blocks = [(rc, ry, rz) for rc in range(plan.nc) for ry in range(plan.ny) for rz in range(plan.nz)]

    def spot(rc, ry, rz):
        shard = (z_at ^ rz) * plan.ny + (y_at + ry) % plan.ny
        return shard, pl.multiple_of(rc * cols + shard * rows, rows)

    for rc, ry, rz in blocks:
        shard, at = spot(rc, ry, rz)
        piece = gates[rc * plan.ny + ry]
        for which, dest in enumerate((wg, wu)):
            loads.append(
                pltpu.make_async_copy(
                    piece.at[rz, pl.ds(which * rows, rows)], dest.at[pl.ds(at, rows)], sem.at[count]
                )
            )
            count += 1
    for rc, ry, rz in blocks:
        shard, at = spot(rc, ry, rz)
        piece = downs[rc * plan.ny + ry]
        late.append(
            pltpu.make_async_copy(piece.at[rz], wd3.at[shard, :, pl.ds(rc * cols, cols)], sem.at[count])
        )
        count += 1
    for copy in loads + late:
        copy.start()
    tokens = xs.shape[0]
    gain = gain_ref[1:2]
    xs[:, lanes - LANES :] = jnp.zeros((tokens, LANES), F32)
    if first:
        xs[:, :width] = x_ref[...].astype(F32)
        mid = xs[...] + dot_nt(attn_ref[...], wo_ref[...])
    else:
        mid = mid_in[...]
    inv = lax.rsqrt(jnp.sum(mid * mid, -1, keepdims=True) * (1.0 / width) + EPS_NORM)
    unit = mid * inv
    normed = (unit * gain).astype(BF16)
    xs[:, :width] = dy_ref[...].astype(F32)
    dy = xs[...].astype(BF16)
    for copy in loads:
        copy.wait()
    gate = dot_nt(normed, wg[...])
    upper = dot_nt(normed, wu[...])
    for copy in late:
        copy.wait()
    units = plan.nc * cols
    wd[width:, :] = jnp.zeros((lanes - width, units), BF16)
    wd[:width, :] = jnp.concatenate([wd3[s].astype(F32) for s in range(plan.shards)], 0).astype(BF16)
    dhidden = dot_nn(dy, wd[...])
    sigma = 1.0 / (1.0 + jnp.exp(-gate))
    act = gate * sigma
    hid = (act * upper).astype(BF16)
    dgate = (dhidden * upper * sigma * (1.0 + gate * (1.0 - sigma))).astype(BF16)
    dupper = (dhidden * act).astype(BF16)
    gg[...] = dot_tn(dgate, normed).astype(BF16)
    gu[...] = dot_tn(dupper, normed).astype(BF16)
    down = dot_tn(dy, hid)
    for s in range(plan.shards):
        gd[s] = down[s * plan.out_rows : (s + 1) * plan.out_rows].astype(BF16)
    stores = []
    count = 0
    for rc, ry, rz in blocks:
        shard, at = spot(rc, ry, rz)
        for which, grad in enumerate((gg, gu)):
            stores.append(
                pltpu.make_async_copy(
                    grad.at[pl.ds(at, rows)], gg_out[rc].at[ry, rz, pl.ds(which * rows, rows)], sem.at[count]
                )
            )
            count += 1
        stores.append(
            pltpu.make_async_copy(gd.at[shard, :, pl.ds(rc * cols, cols)], gd_out[rc].at[ry, rz], sem.at[count])
        )
        count += 1
    for copy in stores:
        copy.start()
    out = (mid if first else out_in[...]) + dot_nt(hid, wd[...])
    dnormed = dot_nn(dgate, wg[...]) + dot_nn(dupper, wu[...])
    if not first:
        dnormed = dnormed + dn_in[...]
    if last:
        out_ref[...] = out[:, :width].astype(BF16)
        total = jnp.sum(dnormed * unit, 0, keepdims=True)
        dgain_ref[...] = jnp.broadcast_to(total, dgain_ref.shape)
        scaled = dnormed * gain
        dmid_ref[...] = (
            inv * (scaled - unit * (jnp.sum(scaled * unit, -1, keepdims=True) * (1.0 / width))) + xs[...]
        )
    else:
        mid_ref[...] = mid
        out_ref[...] = out
        dn_ref[...] = dnormed
    for copy in stores:
        copy.wait()


def backward_in_kernel(dmid_ref, attn_ref, wo_ref, da_ref, grad_ref):
    dmid_b = dmid_ref[...].astype(BF16)
    da_ref[...] = dot_nn(dmid_b, wo_ref[...]).astype(BF16)
    grad_ref[...] = dot_tn(dmid_b, attn_ref[...]).astype(BF16)


def backward_rest_kernel(plan, place, x_ref, dmid_ref, dgain_ref, go_ref, da_ref, attn_ref, q_ref, k_ref, v_ref,
                         prob_ref, wq_ref, wk_ref, wv_ref, gain_ref, cos_ref, sin_ref, dx_ref, *refs):
    packs, refs = refs[: plan.nc], refs[plan.nc :]
    (dq_ref, dkv_ref, pack, xs, sem) = refs
    width, lanes = plan.width, plan.lanes
    x_at, c_at, z_at, y_at = place[0], place[1], place[2], place[3]
    tokens = xs.shape[0]
    n_seq = tokens // SEQUENCE_LENGTH
    cos = cos_ref[...]
    sin = sin_ref[...]

    def unrotate(block):
        return block * cos - swap_halves(block) * sin

    def one_sequence(n, carry):
        at_rows = pl.ds(pl.multiple_of(n * SEQUENCE_LENGTH, SEQUENCE_LENGTH), SEQUENCE_LENGTH)
        dk = [None] * KEY_VALUE_HEADS
        dv = [None] * KEY_VALUE_HEADS
        for pair in range(lanes // LANES):
            at = slice(pair * LANES, (pair + 1) * LANES)
            q2 = q_ref[at_rows, at]
            da2 = da_ref[at_rows, at]
            prod = da2.astype(F32) * attn_ref[at_rows, at].astype(F32)
            total = None
            for odd in range(2):
                h = pair * 2 + odd
                if h >= QUERY_HEADS:
                    continue
                group = h // (QUERY_HEADS // KEY_VALUE_HEADS)
                kf = head_form(k_ref, at_rows, h)
                vf = head_form(v_ref, at_rows, h)
                p = prob_ref[n, h]
                delta = jnp.sum(lane_half(prod, odd), -1, keepdims=True)
                dp = dot_nt(da2, vf)
                ds = (p.astype(F32) * (dp - delta) * HEAD_SIZE ** (-0.5)).astype(BF16)
                part = dot_nn(ds, kf)
                total = part if total is None else total + part
                dvp = dot_tn(p, lane_half(da2, odd))
                dkp = dot_tn(ds, lane_half(q2, odd))
                dv[group] = dvp if dv[group] is None else dv[group] + dvp
                dk[group] = dkp if dk[group] is None else dk[group] + dkp
            dq_ref[at_rows, at] = unrotate(total).astype(BF16)
        for slot, (parts, turn) in enumerate(((dk, unrotate), (dv, lambda b: b))):
            whole = [g + pltpu.roll(g, HEAD_SIZE, 1) for g in parts]
            for b in range(2):
                block = lane_half(whole[2 * b], 0)
                if 2 * b + 1 < KEY_VALUE_HEADS:
                    block = block + lane_half(whole[2 * b + 1], 1)
                dkv_ref[slot, at_rows, b * LANES : (b + 1) * LANES] = turn(block).astype(BF16)
        return carry

    lax.fori_loop(0, n_seq, one_sequence, 0)
    xs[:, lanes - LANES :] = jnp.zeros((tokens, LANES), F32)
    xs[:, :width] = x_ref[...].astype(F32)
    dq, dk, dv = dq_ref[...], dkv_ref[0], dkv_ref[1]
    xfull = xs[...]
    inv = lax.rsqrt(jnp.sum(xfull * xfull, -1, keepdims=True) * (1.0 / width) + EPS_NORM)
    gain = gain_ref[0:1]
    unit = xfull * inv
    normed = (unit * gain).astype(BF16)
    dnormed = dot_nn(dq, wq_ref[...]) + dot_nn(dk, wk_ref[...]) + dot_nn(dv, wv_ref[...])
    lane = lax.broadcasted_iota(jnp.int32, (1, lanes), 1)
    dnormed = jnp.where(lane < width, dnormed, 0.0)
    dgain = jnp.sum(dnormed * unit, 0, keepdims=True)
    grad_q = dot_tn(dq, normed)
    grad_k = dot_tn(dk, normed)
    grad_v = dot_tn(dv, normed)
    grad_out = go_ref[...].astype(F32)
    at = width - (lanes - LANES)
    row = lax.broadcasted_iota(jnp.int32, (LANES, lanes), 0)
    sheet = jnp.where(row == at, dgain, 0.0) + jnp.where(row == at + 1, dgain_ref[0:1], 0.0)
    side = sheet.T
    grad_q = jnp.concatenate([grad_q[:, : lanes - LANES], grad_q[:, lanes - LANES :] + side], 1)
    rows, krows = plan.out_rows, plan.kv_rows
    for s in range(plan.shards):
        a, b = slice(s * rows, (s + 1) * rows), slice(s * krows, (s + 1) * krows)
        pack[0, s] = jnp.concatenate([grad_q[a], grad_k[b]], 0).astype(BF16)
        pack[1, s] = jnp.concatenate([grad_v[b], grad_out[a]], 0).astype(BF16)
    stores = []
    count = 0
    part_rows = plan.half_rows // plan.nx
    for rc in range(2):
        for rx in range(plan.nx):
            for ry in range(plan.ny):
                for rz in range(plan.nz):
                    shard = (z_at ^ rz) * plan.ny + (y_at + ry) % plan.ny
                    half = (c_at + rc) % 2
                    at = pl.multiple_of((x_at + rx) % plan.nx * part_rows, part_rows)
                    target = packs[rc] if plan.nc == 2 else packs[0].at[rc]
                    stores.append(
                        pltpu.make_async_copy(
                            pack.at[half, shard, pl.ds(at, part_rows)], target.at[rx, ry, rz], sem.at[count]
                        )
                    )
                    count += 1
    for copy in stores:
        copy.start()
    scaled = dnormed * gain
    dx = inv * (scaled - unit * (jnp.sum(scaled * unit, -1, keepdims=True) * (1.0 / width))) + dmid_ref[...]
    dx_ref[...] = dx[:, :width].astype(BF16)
    for copy in stores:
        copy.wait()


VMEM = pl.BlockSpec(memory_space=pltpu.VMEM)
SMEM = pl.BlockSpec(memory_space=pltpu.SMEM)
ANY = pl.BlockSpec(memory_space=pl.ANY)


def shape_of(dims, kind):
    return jax.ShapeDtypeStruct(dims, kind)


def cost(micros):
    return pl.CostEstimate(flops=int(micros * 1e9), transcendentals=0, bytes_accessed=int(micros * 1e6))


def attention_forward(plan, place, tokens, cos, sin, pieces):
    rows, lanes = tokens.shape[0], plan.lanes
    n_seq = rows // SEQUENCE_LENGTH
    return pl.pallas_call(
        functools.partial(attention_forward_kernel, plan, len(pieces) // 2),
        name="attention_forward",
        in_specs=[SMEM, VMEM, VMEM, VMEM] + [ANY] * len(pieces),
        out_specs=[VMEM] * 10,
        out_shape=[
            shape_of((rows, lanes), BF16),
            shape_of((rows, 4 * LANES), BF16),
            shape_of((rows, 4 * LANES), BF16),
            shape_of((rows, lanes), BF16),
            shape_of((n_seq, QUERY_HEADS, SEQUENCE_LENGTH, SEQUENCE_LENGTH), BF16),
            shape_of((lanes, lanes), BF16),
            shape_of((2 * LANES, lanes), BF16),
            shape_of((2 * LANES, lanes), BF16),
            shape_of((lanes, lanes), BF16),
            shape_of((8, lanes), F32),
        ],
        scratch_shapes=[
            pltpu.VMEM((2, plan.shards, plan.half_rows, lanes), BF16),
            pltpu.VMEM((rows, lanes), F32),
            pltpu.SemaphoreType.DMA((len(pieces) * plan.nz,)),
        ],
        cost_estimate=cost(10),
    )(place, tokens, cos, sin, *pieces)


def mlp(plan, place, first, last, cotangent, gain, inputs, gates, downs):
    rows, lanes = cotangent.shape[0], plan.lanes
    units = plan.nc * plan.ff_cols
    ff = shape_of((plan.ny, plan.nz, 2 * plan.ff_rows, lanes), BF16)
    dn = shape_of((plan.ny, plan.nz, plan.out_rows, plan.ff_cols), BF16)
    whole = shape_of((rows, lanes), F32)
    results = [shape_of((rows, plan.width), BF16), whole, shape_of((8, lanes), F32)] if last else [whole] * 3
    return pl.pallas_call(
        functools.partial(mlp_kernel, plan, first, last),
        name="mlp",
        in_specs=[SMEM] + [VMEM] * 5 + [ANY] * (len(gates) + len(downs)),
        out_specs=[VMEM] * 3 + [ANY] * (2 * plan.nc),
        out_shape=results + [ff] * plan.nc + [dn] * plan.nc,
        scratch_shapes=[
            pltpu.VMEM((units, lanes), BF16),
            pltpu.VMEM((units, lanes), BF16),
            pltpu.VMEM((plan.shards, plan.out_rows, units), BF16),
            pltpu.VMEM((lanes, units), BF16),
            pltpu.VMEM((units, lanes), BF16),
            pltpu.VMEM((units, lanes), BF16),
            pltpu.VMEM((plan.shards, plan.out_rows, units), BF16),
            pltpu.VMEM((rows, lanes), F32),
            pltpu.SemaphoreType.DMA((3 * plan.shards * plan.nc,)),
        ],
        cost_estimate=cost(12),
    )(place, cotangent, gain, *inputs, *gates, *downs)


def attention_backward(plan, place, tokens, dmid, dgain, attn, q, k, v, prob, wq, wk, wv, wo, gain, cos, sin):
    rows, lanes = tokens.shape[0], plan.lanes
    da, grad_out = pl.pallas_call(
        backward_in_kernel,
        name="backward_in",
        in_specs=[VMEM] * 3,
        out_specs=[VMEM] * 2,
        out_shape=[shape_of((rows, lanes), BF16), shape_of((lanes, lanes), BF16)],
        cost_estimate=cost(4),
    )(dmid, attn, wo)
    block = (plan.nx, plan.ny, plan.nz, plan.half_rows // plan.nx, lanes)
    if plan.nc == 2:
        packs = [shape_of(block, BF16)] * 2
    else:
        packs = [shape_of((2,) + block, BF16)]
    return pl.pallas_call(
        functools.partial(backward_rest_kernel, plan),
        name="backward_rest",
        in_specs=[SMEM] + [VMEM] * 16,
        out_specs=[VMEM] + [ANY] * len(packs),
        out_shape=[shape_of((rows, plan.width), BF16)] + packs,
        scratch_shapes=[
            pltpu.VMEM((rows, lanes), BF16),
            pltpu.VMEM((2, rows, 2 * LANES), BF16),
            pltpu.VMEM((2, plan.shards, plan.half_rows, lanes), BF16),
            pltpu.VMEM((rows, lanes), F32),
            pltpu.SemaphoreType.DMA((2 * plan.nx * plan.shards,)),
        ],
        cost_estimate=cost(14),
    )(place, tokens, dmid, dgain, grad_out, da, attn, q, k, v, prob, wq, wk, wv, gain, cos, sin)


def shift(plan, dim, amount):
    if dim in "xc":
        axis, outer, inner, first = "dp", plan.nx, plan.nc, dim == "x"
    else:
        axis, outer, inner, first = "fsdp", plan.nz, plan.ny, dim == "z"
    pairs = []
    for o in range(outer):
        for i in range(inner):
            if dim == "z":
                to = (o ^ amount, i)
            else:
                to = ((o + amount) % outer, i) if first else (o, (i + amount) % inner)
            pairs.append((o * inner + i, to[0] * inner + to[1]))
    return axis, pairs


def send(plan, value, dim, amount=1):
    axis, pairs = shift(plan, dim, amount)
    return lax.ppermute(value, axis, pairs)


def spread(plan, piece, dims):
    stack = jnp.stack([piece] + [send(plan, piece, "z", k) for k in range(1, plan.nz)])
    held = {(0, 0, 0): stack}
    for dim in dims:
        at = "cxy".index(dim)
        for place, value in list(held.items()):
            place = list(place)
            place[at] = 1
            held[tuple(place)] = send(plan, value, dim)
    return held


def add(a, b):
    return (a.astype(F32) + b.astype(F32)).astype(BF16)


def reduce_z(plan, stack):
    total = stack[0].astype(F32)
    for k in range(1, plan.nz):
        total = total + send(plan, stack[k], "z", k).astype(F32)
    return total.astype(BF16)


def pad_four(results, nc):
    results = list(results)
    return results if nc == 2 else results[:4] + [None, results[4], None]


def layer(plan, tokens, cotangent, w_query, w_key, w_value, w_out, w_gate, w_up, w_down, gain_attn, gain_mlp):
    cos, sin = rope_tables()
    width, lanes, hidden = plan.width, plan.lanes, plan.hidden
    d_at, s_at = lax.axis_index("dp"), lax.axis_index("fsdp")
    if plan.direct:
        place = jnp.stack([d_at // plan.nc, d_at % plan.nc, s_at // plan.ny, s_at % plan.ny]).astype(jnp.int32)
    else:
        place = jnp.zeros((4,), jnp.int32)

    def widen(rows, extra=None):
        rest = lanes - width
        if extra is None:
            return jnp.pad(rows, ((0, 0), (0, rest)))
        side = jnp.pad(extra, ((0, rows.shape[0] - extra.shape[0]), (0, rest - extra.shape[1])))
        return jnp.concatenate([rows, side], 1)

    def all_rows(w):
        return lax.all_gather(w.T, "fsdp", axis=0, tiled=True)

    if plan.direct:
        gains = jnp.stack([gain_attn, gain_mlp], 1)
        first = widen(jnp.concatenate([w_query.T, w_key.T], 0), gains)
        second = widen(jnp.concatenate([w_value.T, w_out.T], 0))
        own = jnp.where(d_at % plan.nc == 0, first, second)
        gate_own = widen(
            jnp.concatenate(
                [lax.dynamic_slice_in_dim(w, d_at * plan.ff_rows, plan.ff_rows, 1).T for w in (w_gate, w_up)], 0
            )
        )
        down_own = w_down.reshape(plan.shards, plan.parts, plan.ff_rows, plan.out_rows)
        down_own = lax.dynamic_index_in_dim(down_own, d_at, 1, False).reshape(plan.ff_cols, plan.out_rows).T
        held = spread(plan, own, "yc")
        pieces = [held[rc, 0, ry] for rc in range(2) for ry in range(2)]
        held_f = spread(plan, gate_own, "xyc")
        held_d = spread(plan, down_own, "yxc")
        keys = [[(rc, rx, ry) for rc in range(plan.nc) for ry in range(plan.ny)] for rx in range(plan.nx)]
        gates = [[held_f[key] for key in part] for part in keys]
        downs = [[held_d[key] for key in part] for part in keys]
    else:
        gains = jnp.stack(
            [lax.all_gather(g, "fsdp", axis=0, tiled=True) for g in (gain_attn, gain_mlp)], 1
        )
        pieces = [
            widen(jnp.concatenate([all_rows(w_query), all_rows(w_key)], 0), gains)[None],
            widen(jnp.concatenate([all_rows(w_value), all_rows(w_out)], 0))[None],
        ]
        gates = [[widen(jnp.concatenate([all_rows(w_gate), all_rows(w_up)], 0))[None]]]
        downs = [[all_rows(w_down)[None]]]

    q, k, v, attn, prob, wq, wk, wv, wo, gain = attention_forward(plan, place, tokens, cos, sin, pieces)
    carried, grads = (tokens, attn, wo), []
    for i in range(plan.nx):
        *carried, gate_a, gate_b, down_a, down_b = pad_four(
            mlp(plan, place, i == 0, i == plan.nx - 1, cotangent, gain, carried, gates[i], downs[i]), plan.nc
        )
        grads.append(((gate_a, gate_b), (down_a, down_b)))
    output, dmid, dgain = carried
    grad_tokens, *packs = attention_backward(
        plan, place, tokens, dmid, dgain, attn, q, k, v, prob, wq, wk, wv, wo, gain, cos, sin
    )
    rows, krows = plan.out_rows, plan.kv_rows

    if plan.direct:

        def fold(pieces, dims):
            mine = [add(a, send(plan, b, "c")) for a, b in pieces]
            away, keep = mine
            if dims == "xy":
                part = add(keep, send(plan, away, "x"))
                part = add(part[0], send(plan, part[1], "y"))
            else:
                both = jnp.stack([keep[1], away[1]])
                got = send(plan, both, "y")
                part = add(add(keep[0], got[0]), send(plan, add(away[0], got[1]), "x"))
            part = reduce_z(plan, part)
            both = jnp.stack([part, send(plan, part, "x")])
            other = send(plan, both, "c")
            quads = jnp.stack([both, other], 1)
            x_at, c_at = d_at // plan.nc, d_at % plan.nc
            quads = jnp.where(c_at == 0, quads, quads[:, ::-1])
            return jnp.where(x_at == 0, quads[::-1], quads)

        def ff(quads):
            return quads.reshape(plan.parts * plan.ff_rows, lanes)[:, :width].astype(F32).T

        ff_rows = plan.ff_rows

        quads = fold([g[0] for g in grads], "xy")
        grad_gate, grad_up = ff(quads[:, :, :ff_rows]), ff(quads[:, :, ff_rows:])
        quads = fold([g[1] for g in grads], "yx")
        quads = quads.reshape(plan.parts, rows, plan.shards, ff_rows)
        grad_down = quads.transpose(2, 0, 3, 1).reshape(hidden, rows).astype(F32)
        got = send(plan, packs[1], "c")
        there = send(plan, add(packs[0][1], got[1]), "x")
        part = add(add(packs[0][0], got[0]), there)
        part = add(part[0], send(plan, part[1], "y"))
        part = reduce_z(plan, part)
        there = send(plan, part, "x")
        x_at, c_at = d_at // plan.nc, d_at % plan.nc
        both = jnp.where(x_at == 0, jnp.concatenate([part, there], 0), jnp.concatenate([there, part], 0))
        other = send(plan, both, "c")
        one = jnp.where(c_at == 0, both, other).astype(F32)
        two = jnp.where(c_at == 0, other, both).astype(F32)
    else:

        def total(value):
            part = lax.psum_scatter(value.astype(F32), "fsdp", scatter_dimension=0, tiled=True)
            return lax.psum(part, "dp")

        both = grads[0][0][0].reshape(2, hidden, lanes)[:, :, :width]
        grad_gate, grad_up = total(both[0]).T, total(both[1]).T
        grad_down = total(grads[0][1][0].reshape(width, hidden)).T
        whole = packs[0].reshape(2, width + plan.kv, lanes)
        one = jnp.concatenate([total(whole[0, :width]), total(whole[0, width:])], 0)
        two = jnp.concatenate([total(whole[1, : plan.kv]), total(whole[1, plan.kv :])], 0)
        rows, krows = width // plan.fsdp, plan.kv // plan.fsdp
    return (
        output,
        grad_tokens,
        one[:rows, :width].T,
        one[rows:, :width].T,
        two[:krows, :width].T,
        two[krows:, :width].T,
        grad_gate,
        grad_up,
        grad_down,
        one[:rows, width],
        one[:rows, width + 1],
    )


def solution(mesh):
    rows = P(("dp", "fsdp"), None)
    cols = P(None, "fsdp")
    one = P("fsdp")

    def run(*args):
        plan = Plan(mesh, args[0].shape[1], args[8].shape[0])
        step = jax.shard_map(
            functools.partial(layer, plan),
            mesh=mesh,
            in_specs=(rows, rows) + (cols,) * 7 + (one, one),
            out_specs=(rows, rows) + (cols,) * 7 + (one, one),
            check_vma=False,
        )
        return step(*args)

    return run
```

```python
import functools

import jax
import jax.numpy as jnp
import numpy as np
from jax import lax
from jax.experimental import pallas as pl
from jax.experimental.pallas import tpu as pltpu
from jax.sharding import PartitionSpec as P


QUERY_HEADS = 9
KEY_VALUE_HEADS = 3
HEAD_SIZE = 64
SEQUENCE_LENGTH = 192

EPS_NORM = 1e-05
ROPE_BASE = 100000.0


F32 = jnp.float32
BF16 = jnp.bfloat16
LANES = 128


def up_to(value, step):
    return -(-value // step) * step


def dot_nn(left, right):
    return lax.dot_general(left, right, (((1,), (0,)), ((), ())), preferred_element_type=F32)


def dot_nt(left, right):
    return lax.dot_general(left, right, (((1,), (1,)), ((), ())), preferred_element_type=F32)


def dot_tn(left, right):
    return lax.dot_general(left, right, (((0,), (0,)), ((), ())), preferred_element_type=F32)


def rope_tables():
    half = HEAD_SIZE // 2
    position = np.arange(SEQUENCE_LENGTH).astype(np.float32)
    freqs = np.power(
        np.float32(ROPE_BASE), -(np.arange(half).astype(np.float32) * np.float32(2.0 / HEAD_SIZE))
    ).astype(np.float32)
    angles = (position[:, None] * freqs[None, :]).astype(np.float32)
    cosine = np.cos(angles.astype(np.float64)).astype(np.float32)
    sine = np.sin(angles.astype(np.float64)).astype(np.float32)
    reps = LANES // HEAD_SIZE
    return (
        jnp.asarray(np.concatenate([cosine, cosine] * reps, 1)),
        jnp.asarray(np.concatenate([-sine, sine] * reps, 1)),
    )


def swap_halves(block):
    half = HEAD_SIZE // 2
    lane = lax.broadcasted_iota(jnp.int32, block.shape, block.ndim - 1)
    return jnp.where(
        lane % HEAD_SIZE < half,
        pltpu.roll(block, LANES - half, block.ndim - 1),
        pltpu.roll(block, half, block.ndim - 1),
    )


def lane_half(block, odd):
    lane = lax.broadcasted_iota(jnp.int32, block.shape, block.ndim - 1)
    keep = (lane >= HEAD_SIZE) if odd else (lane < HEAD_SIZE)
    return jnp.where(keep, block, jnp.zeros_like(block))


class Plan:
    def __init__(self, mesh, width, hidden):
        self.dp, self.fsdp = mesh.shape["dp"], mesh.shape["fsdp"]
        self.width, self.hidden = width, hidden
        self.kv = KEY_VALUE_HEADS * HEAD_SIZE
        self.lanes = up_to(width, LANES)
        self.nx, self.nc = self.dp // 2, 2
        self.nz, self.ny = self.fsdp // 2, 2
        s, d = self.fsdp, self.dp
        self.direct = (
            d == 4
            and s == 8
            and (width // s) % 8 == 0
            and (self.kv // s) % 8 == 0
            and ((width + self.kv) // s) % (16 * (d // 2)) == 0
            and (hidden // s // d) % 16 == 0
            and (hidden // d) % LANES == 0
        )
        if not self.direct:
            self.nx = self.nc = self.nz = self.ny = 1
        self.shards = self.nz * self.ny
        self.parts = self.nx * self.nc
        self.out_rows = width // self.shards
        self.kv_rows = self.kv // self.shards
        self.half_rows = self.out_rows + self.kv_rows
        self.ff_rows = hidden // self.shards // self.parts
        self.ff_cols = hidden // self.parts

    def key(self):
        return (self.dp, self.fsdp, self.width, self.hidden)


def attention_forward_kernel(plan, n_pieces, place, x_ref, cos_ref, sin_ref, *refs):
    pieces, refs = refs[:n_pieces], refs[n_pieces:]
    (q_ref, k_ref, v_ref, attn_ref, prob_ref, wq_ref, wk_ref, wv_ref, wo_ref, gain_ref, pack, xs) = refs
    width, lanes, kv = plan.width, plan.lanes, plan.kv
    x_at, c_at, z_at, y_at = place[0], place[1], place[2], place[3]
    part_rows = plan.half_rows // plan.nx
    spots = [(rc, rx, ry) for rc in range(2) for rx in range(plan.nx) for ry in range(plan.ny)]
    for (rc, rx, ry), piece in zip(spots, pieces):
        half = (c_at + rc) % 2
        at = pl.multiple_of((x_at + rx) % plan.nx * part_rows, part_rows)
        for k in range(plan.nz):
            shard = (z_at ^ k) * plan.ny + (y_at + ry) % plan.ny
            pack[half, shard, pl.ds(at, part_rows)] = piece[k]
    xs[:, lanes - LANES :] = jnp.zeros((xs.shape[0], LANES), F32)
    xs[:, :width] = x_ref[...].astype(F32)
    xfull = xs[...]
    inv = lax.rsqrt(jnp.sum(xfull * xfull, -1, keepdims=True) * (1.0 / width) + EPS_NORM)
    rows, krows = plan.out_rows, plan.kv_rows
    qs, ks, vs, os = [], [], [], []
    for s in range(plan.shards):
        first = pack[0, s].astype(F32)
        second = pack[1, s].astype(F32)
        qs.append(first[:rows])
        ks.append(first[rows:])
        vs.append(second[:krows])
        os.append(second[krows:])
    tail = jnp.zeros((lanes - width, lanes), F32)
    wq_full = jnp.concatenate(qs + [tail], 0)
    lane = lax.broadcasted_iota(jnp.int32, (lanes, lanes), 1)
    wq_ref[...] = jnp.where(lane < width, wq_full, 0.0).astype(BF16)
    kv_pad = 2 * LANES
    ktail = jnp.zeros((kv_pad - kv, lanes), F32)
    wk_ref[...] = jnp.concatenate(ks + [ktail], 0).astype(BF16)
    wv_ref[...] = jnp.concatenate(vs + [ktail], 0).astype(BF16)
    wo_ref[...] = jnp.concatenate(os + [tail], 0).astype(BF16)
    turned = wq_full[:, lanes - LANES :].T
    at = width - (lanes - LANES)
    gain_ref[...] = turned[at : at + 8]
    gain = turned[at : at + 1]
    normed = (xfull * inv * gain).astype(BF16)
    tokens = xs.shape[0]
    n_seq = tokens // SEQUENCE_LENGTH
    cos = cos_ref[...][None]
    sin = sin_ref[...][None]

    def rotate(block):
        cube = block.reshape(n_seq, SEQUENCE_LENGTH, LANES)
        return (cube * cos + swap_halves(cube) * sin).reshape(tokens, LANES)

    q = dot_nt(normed, wq_ref[...])
    for b in range(lanes // LANES):
        q_ref[:, b * LANES : (b + 1) * LANES] = rotate(q[:, b * LANES : (b + 1) * LANES]).astype(BF16)
    k = dot_nt(normed, wk_ref[...])
    v = dot_nt(normed, wv_ref[...])
    for b in range(2):
        kb = rotate(k[:, b * LANES : (b + 1) * LANES])
        vb = v[:, b * LANES : (b + 1) * LANES]
        k_ref[:, b * LANES : (b + 1) * LANES] = kb.astype(BF16)
        v_ref[:, b * LANES : (b + 1) * LANES] = vb.astype(BF16)
        k_ref[:, (b + 2) * LANES : (b + 3) * LANES] = pltpu.roll(kb, HEAD_SIZE, 1).astype(BF16)
        v_ref[:, (b + 2) * LANES : (b + 3) * LANES] = pltpu.roll(vb, HEAD_SIZE, 1).astype(BF16)

    shape = (SEQUENCE_LENGTH, SEQUENCE_LENGTH)
    allowed = lax.broadcasted_iota(jnp.int32, shape, 0) >= lax.broadcasted_iota(jnp.int32, shape, 1)

    def one_sequence(n, carry):
        at_rows = pl.ds(pl.multiple_of(n * SEQUENCE_LENGTH, SEQUENCE_LENGTH), SEQUENCE_LENGTH)
        for pair in range(lanes // LANES):
            q2 = q_ref[at_rows, pair * LANES : (pair + 1) * LANES]
            total = None
            for odd in range(2):
                h = pair * 2 + odd
                if h >= QUERY_HEADS:
                    continue
                kf = head_form(k_ref, at_rows, h)
                vf = head_form(v_ref, at_rows, h)
                scores = dot_nt(q2, kf) * HEAD_SIZE ** (-0.5)
                expo = jnp.where(allowed, jnp.exp(jnp.where(allowed, scores, 0.0)), 0.0)
                p = (expo * (1.0 / jnp.sum(expo, -1, keepdims=True))).astype(BF16)
                prob_ref[n, h] = p
                part = dot_nn(p, vf)
                total = part if total is None else total + part
            attn_ref[at_rows, pair * LANES : (pair + 1) * LANES] = total.astype(BF16)
        return carry

    lax.fori_loop(0, n_seq, one_sequence, 0)


def head_form(ref, at_rows, h):
    group, odd = h // (QUERY_HEADS // KEY_VALUE_HEADS), h % 2
    block = group // 2 + (2 if group % 2 != odd else 0)
    return lane_half(ref[at_rows, block * LANES : (block + 1) * LANES], odd)


def mlp_kernel(plan, first, last, place, dy_ref, gain_ref, *refs):
    if first:
        x_ref, attn_ref, wo_ref, refs = refs[0], refs[1], refs[2], refs[3:]
    else:
        mid_in, out_in, dn_in, refs = refs[0], refs[1], refs[2], refs[3:]
    n_pieces = plan.nc * plan.ny
    gates, refs = refs[:n_pieces], refs[n_pieces:]
    downs, refs = refs[:n_pieces], refs[n_pieces:]
    if last:
        out_ref, dmid_ref, dgain_ref, refs = refs[0], refs[1], refs[2], refs[3:]
    else:
        mid_ref, out_ref, dn_ref, refs = refs[0], refs[1], refs[2], refs[3:]
    gg_out, refs = refs[: plan.nc], refs[plan.nc :]
    gd_out, refs = refs[: plan.nc], refs[plan.nc :]
    (wg, wu, wd3, wd, gg, gu, gd, xs) = refs
    width, lanes = plan.width, plan.lanes
    z_at, y_at = place[2], place[3]
    rows, cols = plan.ff_rows, plan.ff_cols
    blocks = [(rc, ry, rz) for rc in range(plan.nc) for ry in range(plan.ny) for rz in range(plan.nz)]

    def spot(rc, ry, rz):
        shard = (z_at ^ rz) * plan.ny + (y_at + ry) % plan.ny
        return shard, pl.ds(pl.multiple_of(rc * cols + shard * rows, rows), rows)

    for rc, ry, rz in blocks:
        shard, at = spot(rc, ry, rz)
        piece = gates[rc * plan.ny + ry]
        wg[at, :] = piece[rz, :rows]
        wu[at, :] = piece[rz, rows:]
        wd3[shard, :, rc * cols : (rc + 1) * cols] = downs[rc * plan.ny + ry][rz]
    tokens = xs.shape[0]
    gain = gain_ref[1:2]
    xs[:, lanes - LANES :] = jnp.zeros((tokens, LANES), F32)
    if first:
        xs[:, :width] = x_ref[...].astype(F32)
        mid = xs[...] + dot_nt(attn_ref[...], wo_ref[...])
    else:
        mid = mid_in[...]
    inv = lax.rsqrt(jnp.sum(mid * mid, -1, keepdims=True) * (1.0 / width) + EPS_NORM)
    unit = mid * inv
    normed = (unit * gain).astype(BF16)
    xs[:, :width] = dy_ref[...].astype(F32)
    dy = xs[...].astype(BF16)
    gate = dot_nt(normed, wg[...])
    upper = dot_nt(normed, wu[...])
    units = plan.nc * cols
    wd[width:, :] = jnp.zeros((lanes - width, units), BF16)
    wd[:width, :] = jnp.concatenate([wd3[s].astype(F32) for s in range(plan.shards)], 0).astype(BF16)
    dhidden = dot_nn(dy, wd[...])
    sigma = 1.0 / (1.0 + jnp.exp(-gate))
    act = gate * sigma
    hid = (act * upper).astype(BF16)
    dgate = (dhidden * upper * sigma * (1.0 + gate * (1.0 - sigma))).astype(BF16)
    dupper = (dhidden * act).astype(BF16)
    gg[...] = dot_tn(dgate, normed).astype(BF16)
    gu[...] = dot_tn(dupper, normed).astype(BF16)
    down = dot_tn(dy, hid)
    for s in range(plan.shards):
        gd[s] = down[s * plan.out_rows : (s + 1) * plan.out_rows].astype(BF16)
    for rc, ry, rz in blocks:
        shard, at = spot(rc, ry, rz)
        gg_out[rc][ry, rz, :rows] = gg[at, :]
        gg_out[rc][ry, rz, rows:] = gu[at, :]
        gd_out[rc][ry, rz] = gd[shard, :, rc * cols : (rc + 1) * cols]
    out = (mid if first else out_in[...]) + dot_nt(hid, wd[...])
    dnormed = dot_nn(dgate, wg[...]) + dot_nn(dupper, wu[...])
    if not first:
        dnormed = dnormed + dn_in[...]
    if last:
        out_ref[...] = out[:, :width].astype(BF16)
        total = jnp.sum(dnormed * unit, 0, keepdims=True)
        dgain_ref[...] = jnp.broadcast_to(total, dgain_ref.shape)
        scaled = dnormed * gain
        dmid_ref[...] = (
            inv * (scaled - unit * (jnp.sum(scaled * unit, -1, keepdims=True) * (1.0 / width))) + xs[...]
        )
    else:
        mid_ref[...] = mid
        out_ref[...] = out
        dn_ref[...] = dnormed


def backward_in_kernel(dmid_ref, attn_ref, wo_ref, da_ref, grad_ref):
    dmid_b = dmid_ref[...].astype(BF16)
    da_ref[...] = dot_nn(dmid_b, wo_ref[...]).astype(BF16)
    grad_ref[...] = dot_tn(dmid_b, attn_ref[...]).astype(BF16)


def backward_rest_kernel(plan, place, x_ref, dmid_ref, dgain_ref, go_ref, da_ref, attn_ref, q_ref, k_ref, v_ref,
                         prob_ref, wq_ref, wk_ref, wv_ref, gain_ref, cos_ref, sin_ref, dx_ref, *refs):
    packs, refs = refs[: plan.nc], refs[plan.nc :]
    (dq_ref, dkv_ref, pack, xs) = refs
    width, lanes = plan.width, plan.lanes
    x_at, c_at, z_at, y_at = place[0], place[1], place[2], place[3]
    tokens = xs.shape[0]
    n_seq = tokens // SEQUENCE_LENGTH
    cos = cos_ref[...]
    sin = sin_ref[...]

    def unrotate(block):
        return block * cos - swap_halves(block) * sin

    def one_sequence(n, carry):
        at_rows = pl.ds(pl.multiple_of(n * SEQUENCE_LENGTH, SEQUENCE_LENGTH), SEQUENCE_LENGTH)
        dk = [None] * KEY_VALUE_HEADS
        dv = [None] * KEY_VALUE_HEADS
        for pair in range(lanes // LANES):
            at = slice(pair * LANES, (pair + 1) * LANES)
            q2 = q_ref[at_rows, at]
            da2 = da_ref[at_rows, at]
            prod = da2.astype(F32) * attn_ref[at_rows, at].astype(F32)
            total = None
            for odd in range(2):
                h = pair * 2 + odd
                if h >= QUERY_HEADS:
                    continue
                group = h // (QUERY_HEADS // KEY_VALUE_HEADS)
                kf = head_form(k_ref, at_rows, h)
                vf = head_form(v_ref, at_rows, h)
                p = prob_ref[n, h]
                delta = jnp.sum(lane_half(prod, odd), -1, keepdims=True)
                dp = dot_nt(da2, vf)
                ds = (p.astype(F32) * (dp - delta) * HEAD_SIZE ** (-0.5)).astype(BF16)
                part = dot_nn(ds, kf)
                total = part if total is None else total + part
                dvp = dot_tn(p, lane_half(da2, odd))
                dkp = dot_tn(ds, lane_half(q2, odd))
                dv[group] = dvp if dv[group] is None else dv[group] + dvp
                dk[group] = dkp if dk[group] is None else dk[group] + dkp
            dq_ref[at_rows, at] = unrotate(total).astype(BF16)
        for slot, (parts, turn) in enumerate(((dk, unrotate), (dv, lambda b: b))):
            whole = [g + pltpu.roll(g, HEAD_SIZE, 1) for g in parts]
            for b in range(2):
                block = lane_half(whole[2 * b], 0)
                if 2 * b + 1 < KEY_VALUE_HEADS:
                    block = block + lane_half(whole[2 * b + 1], 1)
                dkv_ref[slot, at_rows, b * LANES : (b + 1) * LANES] = turn(block).astype(BF16)
        return carry

    lax.fori_loop(0, n_seq, one_sequence, 0)
    xs[:, lanes - LANES :] = jnp.zeros((tokens, LANES), F32)
    xs[:, :width] = x_ref[...].astype(F32)
    dq, dk, dv = dq_ref[...], dkv_ref[0], dkv_ref[1]
    xfull = xs[...]
    inv = lax.rsqrt(jnp.sum(xfull * xfull, -1, keepdims=True) * (1.0 / width) + EPS_NORM)
    gain = gain_ref[0:1]
    unit = xfull * inv
    normed = (unit * gain).astype(BF16)
    dnormed = dot_nn(dq, wq_ref[...]) + dot_nn(dk, wk_ref[...]) + dot_nn(dv, wv_ref[...])
    lane = lax.broadcasted_iota(jnp.int32, (1, lanes), 1)
    dnormed = jnp.where(lane < width, dnormed, 0.0)
    dgain = jnp.sum(dnormed * unit, 0, keepdims=True)
    grad_q = dot_tn(dq, normed)
    grad_k = dot_tn(dk, normed)
    grad_v = dot_tn(dv, normed)
    grad_out = go_ref[...].astype(F32)
    at = width - (lanes - LANES)
    row = lax.broadcasted_iota(jnp.int32, (LANES, lanes), 0)
    sheet = jnp.where(row == at, dgain, 0.0) + jnp.where(row == at + 1, dgain_ref[0:1], 0.0)
    side = sheet.T
    grad_q = jnp.concatenate([grad_q[:, : lanes - LANES], grad_q[:, lanes - LANES :] + side], 1)
    rows, krows = plan.out_rows, plan.kv_rows
    for s in range(plan.shards):
        a, b = slice(s * rows, (s + 1) * rows), slice(s * krows, (s + 1) * krows)
        pack[0, s] = jnp.concatenate([grad_q[a], grad_k[b]], 0).astype(BF16)
        pack[1, s] = jnp.concatenate([grad_v[b], grad_out[a]], 0).astype(BF16)
    part_rows = plan.half_rows // plan.nx
    for rc in range(2):
        for rx in range(plan.nx):
            for ry in range(plan.ny):
                for rz in range(plan.nz):
                    shard = (z_at ^ rz) * plan.ny + (y_at + ry) % plan.ny
                    at = pl.multiple_of((x_at + rx) % plan.nx * part_rows, part_rows)
                    block = pack[(c_at + rc) % 2, shard, pl.ds(at, part_rows)]
                    if plan.nc == 2:
                        packs[rc][rx, ry, rz] = block
                    else:
                        packs[0][rc, rx, ry, rz] = block
    scaled = dnormed * gain
    dx = inv * (scaled - unit * (jnp.sum(scaled * unit, -1, keepdims=True) * (1.0 / width))) + dmid_ref[...]
    dx_ref[...] = dx[:, :width].astype(BF16)


VMEM = pl.BlockSpec(memory_space=pltpu.VMEM)
SMEM = pl.BlockSpec(memory_space=pltpu.SMEM)


def shape_of(dims, kind):
    return jax.ShapeDtypeStruct(dims, kind)


def limit(plan, mib):
    return pltpu.CompilerParams(vmem_limit_bytes=(mib if plan.direct else 60) * 2**20)


def kept(plan):
    return pltpu.VMEM if plan.direct else shape_of


def cost(micros):
    return pl.CostEstimate(flops=int(micros * 1e9), transcendentals=0, bytes_accessed=int(micros * 1e6))


def attention_forward(plan, place, tokens, cos, sin, pieces):
    rows, lanes = tokens.shape[0], plan.lanes
    n_seq = rows // SEQUENCE_LENGTH
    held = kept(plan)
    return pl.pallas_call(
        functools.partial(attention_forward_kernel, plan, len(pieces)),
        name="attention_forward",
        in_specs=[SMEM] + [VMEM] * (3 + len(pieces)),
        out_specs=[VMEM] * 10,
        out_shape=[
            held((rows, lanes), BF16),
            held((rows, 4 * LANES), BF16),
            held((rows, 4 * LANES), BF16),
            held((rows, lanes), BF16),
            held((n_seq, QUERY_HEADS, SEQUENCE_LENGTH, SEQUENCE_LENGTH), BF16),
            held((lanes, lanes), BF16),
            held((2 * LANES, lanes), BF16),
            held((2 * LANES, lanes), BF16),
            held((lanes, lanes), BF16),
            held((8, lanes), F32),
        ],
        scratch_shapes=[
            pltpu.VMEM((2, plan.shards, plan.half_rows, lanes), BF16),
            pltpu.VMEM((rows, lanes), F32),
        ],
        cost_estimate=cost(10),
            compiler_params=limit(plan, 12),
    )(place, tokens, cos, sin, *pieces)


def mlp(plan, place, first, last, cotangent, gain, inputs, gates, downs):
    rows, lanes = cotangent.shape[0], plan.lanes
    held = kept(plan)
    units = plan.nc * plan.ff_cols
    ff = held((plan.ny, plan.nz, 2 * plan.ff_rows, lanes), BF16)
    dn = held((plan.ny, plan.nz, plan.out_rows, plan.ff_cols), BF16)
    whole = held((rows, lanes), F32)
    results = [shape_of((rows, plan.width), BF16), whole, held((8, lanes), F32)] if last else [whole] * 3
    return pl.pallas_call(
        functools.partial(mlp_kernel, plan, first, last),
        name="mlp",
        in_specs=[SMEM] + [VMEM] * (5 + len(gates) + len(downs)),
        out_specs=[VMEM] * (3 + 2 * plan.nc),
        out_shape=results + [ff] * plan.nc + [dn] * plan.nc,
        scratch_shapes=[
            pltpu.VMEM((units, lanes), BF16),
            pltpu.VMEM((units, lanes), BF16),
            pltpu.VMEM((plan.shards, plan.out_rows, units), BF16),
            pltpu.VMEM((lanes, units), BF16),
            pltpu.VMEM((units, lanes), BF16),
            pltpu.VMEM((units, lanes), BF16),
            pltpu.VMEM((plan.shards, plan.out_rows, units), BF16),
            pltpu.VMEM((rows, lanes), F32),
        ],
        cost_estimate=cost(12),
            compiler_params=limit(plan, 24),
    )(place, cotangent, gain, *inputs, *gates, *downs)


def attention_backward(plan, place, tokens, dmid, dgain, attn, q, k, v, prob, wq, wk, wv, wo, gain, cos, sin):
    rows, lanes = tokens.shape[0], plan.lanes
    held = kept(plan)
    da, grad_out = pl.pallas_call(
        backward_in_kernel,
        name="backward_in",
        in_specs=[VMEM] * 3,
        out_specs=[VMEM] * 2,
        out_shape=[held((rows, lanes), BF16), held((lanes, lanes), BF16)],
        cost_estimate=cost(4),
        compiler_params=limit(plan, 6),
    )(dmid, attn, wo)
    block = (plan.nx, plan.ny, plan.nz, plan.half_rows // plan.nx, lanes)
    if plan.nc == 2:
        packs = [held(block, BF16)] * 2
    else:
        packs = [shape_of((2,) + block, BF16)]
    return pl.pallas_call(
        functools.partial(backward_rest_kernel, plan),
        name="backward_rest",
        in_specs=[SMEM] + [VMEM] * 16,
        out_specs=[VMEM] * (1 + len(packs)),
        out_shape=[shape_of((rows, plan.width), BF16)] + packs,
        scratch_shapes=[
            pltpu.VMEM((rows, lanes), BF16),
            pltpu.VMEM((2, rows, 2 * LANES), BF16),
            pltpu.VMEM((2, plan.shards, plan.half_rows, lanes), BF16),
            pltpu.VMEM((rows, lanes), F32),
        ],
        cost_estimate=cost(14),
        compiler_params=limit(plan, 16),
    )(place, tokens, dmid, dgain, grad_out, da, attn, q, k, v, prob, wq, wk, wv, gain, cos, sin)


def shift(plan, dim, amount):
    if dim in "xc":
        axis, outer, inner, first = "dp", plan.nx, plan.nc, dim == "x"
    else:
        axis, outer, inner, first = "fsdp", plan.nz, plan.ny, dim == "z"
    pairs = []
    for o in range(outer):
        for i in range(inner):
            if dim == "z":
                to = (o ^ amount, i)
            else:
                to = ((o + amount) % outer, i) if first else (o, (i + amount) % inner)
            pairs.append((o * inner + i, to[0] * inner + to[1]))
    return axis, pairs


def send(plan, value, dim, amount=1):
    axis, pairs = shift(plan, dim, amount)
    return lax.ppermute(value, axis, pairs)


def spread(plan, piece, dims):
    stack = jnp.stack([piece] + [send(plan, piece, "z", k) for k in range(1, plan.nz)])
    held = {(0, 0, 0): stack}
    for dim in dims:
        at = "cxy".index(dim)
        for place, value in list(held.items()):
            place = list(place)
            place[at] = 1
            held[tuple(place)] = send(plan, value, dim)
    return held


def add(a, b):
    return (a.astype(F32) + b.astype(F32)).astype(BF16)


def reduce_z(plan, stack):
    total = stack[0].astype(F32)
    for k in range(1, plan.nz):
        total = total + send(plan, stack[k], "z", k).astype(F32)
    return total.astype(BF16)


def pad_four(results, nc):
    results = list(results)
    return results if nc == 2 else results[:4] + [None, results[4], None]


def layer(plan, tokens, cotangent, w_query, w_key, w_value, w_out, w_gate, w_up, w_down, gain_attn, gain_mlp):
    cos, sin = rope_tables()
    width, lanes, hidden = plan.width, plan.lanes, plan.hidden
    d_at, s_at = lax.axis_index("dp"), lax.axis_index("fsdp")
    if plan.direct:
        x_at, c_at = d_at // plan.nc, d_at % plan.nc
        place = jnp.stack([x_at, c_at, s_at // plan.ny, s_at % plan.ny]).astype(jnp.int32)
        place, x_first, c_first, ff_at, d_at, w_query = lax.optimization_barrier(
            (place, x_at == 0, c_at == 0, d_at * plan.ff_rows, d_at, w_query)
        )
    else:
        place = jnp.zeros((4,), jnp.int32)

    def widen(rows, extra=None):
        rest = lanes - width
        if extra is None:
            return jnp.pad(rows, ((0, 0), (0, rest)))
        side = jnp.pad(extra, ((0, rows.shape[0] - extra.shape[0]), (0, rest - extra.shape[1])))
        return jnp.concatenate([rows, side], 1)

    def all_rows(w):
        return lax.all_gather(w.T, "fsdp", axis=0, tiled=True)

    if plan.direct:
        gains = jnp.stack([gain_attn, gain_mlp], 1)
        first = widen(jnp.concatenate([w_query.T, w_key.T], 0), gains)
        second = widen(jnp.concatenate([w_value.T, w_out.T], 0))
        own = jnp.where(c_first, first, second)
        part_rows = plan.half_rows // plan.nx
        own = jnp.where(x_first, own[:part_rows], own[part_rows:])
        gate_own = widen(
            jnp.concatenate(
                [lax.dynamic_slice_in_dim(w, ff_at, plan.ff_rows, 1).T for w in (w_gate, w_up)], 0
            )
        )
        down_own = w_down.reshape(plan.shards, plan.parts, plan.ff_rows, plan.out_rows)
        down_own = lax.dynamic_index_in_dim(down_own, d_at, 1, False).reshape(plan.ff_cols, plan.out_rows).T
        held_a = spread(plan, own, "yxc")
        spots = [(rc, rx, ry) for rc in range(plan.nc) for rx in range(plan.nx) for ry in range(plan.ny)]
        pieces = [held_a[spot] for spot in spots]
        held_f = spread(plan, gate_own, "xyc")
        held_d = spread(plan, down_own, "yxc")
        keys = [[(rc, rx, ry) for rc in range(plan.nc) for ry in range(plan.ny)] for rx in range(plan.nx)]
        gates = [[held_f[key] for key in part] for part in keys]
        downs = [[held_d[key] for key in part] for part in keys]
    else:
        gains = jnp.stack(
            [lax.all_gather(g, "fsdp", axis=0, tiled=True) for g in (gain_attn, gain_mlp)], 1
        )
        pieces = [
            widen(jnp.concatenate([all_rows(w_query), all_rows(w_key)], 0), gains)[None],
            widen(jnp.concatenate([all_rows(w_value), all_rows(w_out)], 0))[None],
        ]
        gates = [[widen(jnp.concatenate([all_rows(w_gate), all_rows(w_up)], 0))[None]]]
        downs = [[all_rows(w_down)[None]]]

    q, k, v, attn, prob, wq, wk, wv, wo, gain = attention_forward(plan, place, tokens, cos, sin, pieces)
    carried, grads = (tokens, attn, wo), []
    for i in range(plan.nx):
        *carried, gate_a, gate_b, down_a, down_b = pad_four(
            mlp(plan, place, i == 0, i == plan.nx - 1, cotangent, gain, carried, gates[i], downs[i]), plan.nc
        )
        grads.append(((gate_a, gate_b), (down_a, down_b)))
    output, dmid, dgain = carried
    grad_tokens, *packs = attention_backward(
        plan, place, tokens, dmid, dgain, attn, q, k, v, prob, wq, wk, wv, wo, gain, cos, sin
    )
    rows, krows = plan.out_rows, plan.kv_rows

    if plan.direct:

        def fold(pieces, dims):
            mine = [add(a, send(plan, b, "c")) for a, b in pieces]
            away, keep = mine
            if dims == "xy":
                part = add(keep, send(plan, away, "x"))
                part = add(part[0], send(plan, part[1], "y"))
            else:
                both = jnp.stack([keep[1], away[1]])
                got = send(plan, both, "y")
                part = add(add(keep[0], got[0]), send(plan, add(away[0], got[1]), "x"))
            part = reduce_z(plan, part)
            both = jnp.stack([part, send(plan, part, "x")])
            other = send(plan, both, "c")
            quads = jnp.stack([both, other], 1)
            quads = jnp.where(c_first, quads, quads[:, ::-1])
            return jnp.where(x_first, quads[::-1], quads)

        def ff(quads):
            return quads.reshape(plan.parts * plan.ff_rows, lanes)[:, :width].astype(F32).T

        ff_rows = plan.ff_rows

        quads = fold([g[0] for g in grads], "xy")
        grad_gate, grad_up = ff(quads[:, :, :ff_rows]), ff(quads[:, :, ff_rows:])
        quads = fold([g[1] for g in grads], "yx")
        quads = quads.reshape(plan.parts, rows, plan.shards, ff_rows)
        grad_down = quads.transpose(2, 0, 3, 1).reshape(hidden, rows).astype(F32)
        got = send(plan, packs[1], "c")
        there = send(plan, add(packs[0][1], got[1]), "x")
        part = add(add(packs[0][0], got[0]), there)
        part = add(part[0], send(plan, part[1], "y"))
        part = reduce_z(plan, part)
        there = send(plan, part, "x")
        both = jnp.where(x_first, jnp.concatenate([part, there], 0), jnp.concatenate([there, part], 0))
        other = send(plan, both, "c")
        one = jnp.where(c_first, both, other).astype(F32)
        two = jnp.where(c_first, other, both).astype(F32)
    else:

        def total(value):
            part = lax.psum_scatter(value.astype(F32), "fsdp", scatter_dimension=0, tiled=True)
            return lax.psum(part, "dp")

        both = grads[0][0][0].reshape(2, hidden, lanes)[:, :, :width]
        grad_gate, grad_up = total(both[0]).T, total(both[1]).T
        grad_down = total(grads[0][1][0].reshape(width, hidden)).T
        whole = packs[0].reshape(2, width + plan.kv, lanes)
        one = jnp.concatenate([total(whole[0, :width]), total(whole[0, width:])], 0)
        two = jnp.concatenate([total(whole[1, : plan.kv]), total(whole[1, plan.kv :])], 0)
        rows, krows = width // plan.fsdp, plan.kv // plan.fsdp
    return (
        output,
        grad_tokens,
        one[:rows, :width].T,
        one[rows:, :width].T,
        two[:krows, :width].T,
        two[krows:, :width].T,
        grad_gate,
        grad_up,
        grad_down,
        one[:rows, width],
        one[:rows, width + 1],
    )


def solution(mesh):
    rows = P(("dp", "fsdp"), None)
    cols = P(None, "fsdp")
    one = P("fsdp")

    def run(*args):
        plan = Plan(mesh, args[0].shape[1], args[8].shape[0])
        step = jax.shard_map(
            functools.partial(layer, plan),
            mesh=mesh,
            in_specs=(rows, rows) + (cols,) * 7 + (one, one),
            out_specs=(rows, rows) + (cols,) * 7 + (one, one),
            check_vma=False,
        )
        return step(*args)

    return run
```

```python
import functools

import jax
import jax.numpy as jnp
import numpy as np
from jax import lax
from jax.experimental import pallas as pl
from jax.experimental.pallas import tpu as pltpu
from jax.sharding import PartitionSpec as P


QUERY_HEADS = 9
KEY_VALUE_HEADS = 3
HEAD_SIZE = 64
SEQUENCE_LENGTH = 192

EPS_NORM = 1e-05
ROPE_BASE = 100000.0


F32 = jnp.float32
BF16 = jnp.bfloat16
LANES = 128


def up_to(value, step):
    return -(-value // step) * step


def dot_nn(left, right):
    return lax.dot_general(left, right, (((1,), (0,)), ((), ())), preferred_element_type=F32)


def dot_nt(left, right):
    return lax.dot_general(left, right, (((1,), (1,)), ((), ())), preferred_element_type=F32)


def dot_tn(left, right):
    return lax.dot_general(left, right, (((0,), (0,)), ((), ())), preferred_element_type=F32)


def rope_tables():
    half = HEAD_SIZE // 2
    position = np.arange(SEQUENCE_LENGTH).astype(np.float32)
    freqs = np.power(
        np.float32(ROPE_BASE), -(np.arange(half).astype(np.float32) * np.float32(2.0 / HEAD_SIZE))
    ).astype(np.float32)
    angles = (position[:, None] * freqs[None, :]).astype(np.float32)
    cosine = np.cos(angles.astype(np.float64)).astype(np.float32)
    sine = np.sin(angles.astype(np.float64)).astype(np.float32)
    reps = LANES // HEAD_SIZE
    return (
        jnp.asarray(np.concatenate([cosine, cosine] * reps, 1)),
        jnp.asarray(np.concatenate([-sine, sine] * reps, 1)),
    )


def swap_halves(block):
    half = HEAD_SIZE // 2
    lane = lax.broadcasted_iota(jnp.int32, block.shape, block.ndim - 1)
    return jnp.where(
        lane % HEAD_SIZE < half,
        pltpu.roll(block, LANES - half, block.ndim - 1),
        pltpu.roll(block, half, block.ndim - 1),
    )


def lane_half(block, odd):
    lane = lax.broadcasted_iota(jnp.int32, block.shape, block.ndim - 1)
    keep = (lane >= HEAD_SIZE) if odd else (lane < HEAD_SIZE)
    return jnp.where(keep, block, jnp.zeros_like(block))


class Plan:
    def __init__(self, mesh, width, hidden):
        self.dp, self.fsdp = mesh.shape["dp"], mesh.shape["fsdp"]
        self.width, self.hidden = width, hidden
        self.kv = KEY_VALUE_HEADS * HEAD_SIZE
        self.lanes = up_to(width, LANES)
        self.nx, self.nc = self.dp // 2, 2
        self.nz, self.ny = self.fsdp // 2, 2
        s, d = self.fsdp, self.dp
        self.direct = (
            d == 4
            and s == 8
            and (width // s) % 8 == 0
            and (self.kv // s) % 8 == 0
            and ((width + self.kv) // s) % (16 * (d // 2)) == 0
            and (hidden // s // d) % 16 == 0
            and (hidden // d) % LANES == 0
        )
        if not self.direct:
            self.nx = self.nc = self.nz = self.ny = 1
        self.shards = self.nz * self.ny
        self.parts = self.nx * self.nc
        self.out_rows = width // self.shards
        self.kv_rows = self.kv // self.shards
        self.half_rows = self.out_rows + self.kv_rows
        self.ff_rows = hidden // self.shards // self.parts
        self.ff_cols = hidden // self.parts

    def key(self):
        return (self.dp, self.fsdp, self.width, self.hidden)


def attention_forward_kernel(plan, n_pieces, place, x_ref, cos_ref, sin_ref, *refs):
    pieces, refs = refs[:n_pieces], refs[n_pieces:]
    (q_ref, k_ref, v_ref, attn_ref, prob_ref, wq_ref, wk_ref, wv_ref, wo_ref, gain_ref, pack, xs) = refs
    width, lanes, kv = plan.width, plan.lanes, plan.kv
    x_at, c_at, z_at, y_at = place[0], place[1], place[2], place[3]
    part_rows = plan.half_rows // plan.nx
    spots = [(rc, rx, ry) for rc in range(2) for rx in range(plan.nx) for ry in range(plan.ny)]
    for (rc, rx, ry), piece in zip(spots, pieces):
        half = (c_at + rc) % 2
        at = pl.multiple_of((x_at + rx) % plan.nx * part_rows, part_rows)
        for k in range(plan.nz):
            shard = (z_at ^ k) * plan.ny + (y_at + ry) % plan.ny
            pack[half, shard, pl.ds(at, part_rows)] = piece[k]
    xs[:, lanes - LANES :] = jnp.zeros((xs.shape[0], LANES), F32)
    xs[:, :width] = x_ref[...].astype(F32)
    xfull = xs[...]
    inv = lax.rsqrt(jnp.sum(xfull * xfull, -1, keepdims=True) * (1.0 / width) + EPS_NORM)
    rows, krows = plan.out_rows, plan.kv_rows
    qs, ks, vs, os = [], [], [], []
    for s in range(plan.shards):
        first = pack[0, s].astype(F32)
        second = pack[1, s].astype(F32)
        qs.append(first[:rows])
        ks.append(first[rows:])
        vs.append(second[:krows])
        os.append(second[krows:])
    tail = jnp.zeros((lanes - width, lanes), F32)
    wq_full = jnp.concatenate(qs + [tail], 0)
    lane = lax.broadcasted_iota(jnp.int32, (lanes, lanes), 1)
    wq_ref[...] = jnp.where(lane < width, wq_full, 0.0).astype(BF16)
    kv_pad = 2 * LANES
    ktail = jnp.zeros((kv_pad - kv, lanes), F32)
    wk_ref[...] = jnp.concatenate(ks + [ktail], 0).astype(BF16)
    wv_ref[...] = jnp.concatenate(vs + [ktail], 0).astype(BF16)
    wo_ref[...] = jnp.concatenate(os + [tail], 0).astype(BF16)
    turned = wq_full[:, lanes - LANES :].T
    at = width - (lanes - LANES)
    gain_ref[...] = turned[at : at + 8]
    gain = turned[at : at + 1]
    normed = (xfull * inv * gain).astype(BF16)
    tokens = xs.shape[0]
    n_seq = tokens // SEQUENCE_LENGTH
    cos = cos_ref[...][None]
    sin = sin_ref[...][None]

    def rotate(block):
        cube = block.reshape(n_seq, SEQUENCE_LENGTH, LANES)
        return (cube * cos + swap_halves(cube) * sin).reshape(tokens, LANES)

    q = dot_nt(normed, wq_ref[...])
    for b in range(lanes // LANES):
        q_ref[:, b * LANES : (b + 1) * LANES] = rotate(q[:, b * LANES : (b + 1) * LANES]).astype(BF16)
    k = dot_nt(normed, wk_ref[...])
    v = dot_nt(normed, wv_ref[...])
    for b in range(2):
        kb = rotate(k[:, b * LANES : (b + 1) * LANES])
        vb = v[:, b * LANES : (b + 1) * LANES]
        k_ref[:, b * LANES : (b + 1) * LANES] = kb.astype(BF16)
        v_ref[:, b * LANES : (b + 1) * LANES] = vb.astype(BF16)
        k_ref[:, (b + 2) * LANES : (b + 3) * LANES] = pltpu.roll(kb, HEAD_SIZE, 1).astype(BF16)
        v_ref[:, (b + 2) * LANES : (b + 3) * LANES] = pltpu.roll(vb, HEAD_SIZE, 1).astype(BF16)

    shape = (SEQUENCE_LENGTH, SEQUENCE_LENGTH)
    allowed = lax.broadcasted_iota(jnp.int32, shape, 0) >= lax.broadcasted_iota(jnp.int32, shape, 1)

    def one_sequence(n, carry):
        at_rows = pl.ds(pl.multiple_of(n * SEQUENCE_LENGTH, SEQUENCE_LENGTH), SEQUENCE_LENGTH)
        for pair in range(lanes // LANES):
            q2 = q_ref[at_rows, pair * LANES : (pair + 1) * LANES]
            total = None
            for odd in range(2):
                h = pair * 2 + odd
                if h >= QUERY_HEADS:
                    continue
                kf = head_form(k_ref, at_rows, h)
                vf = head_form(v_ref, at_rows, h)
                scores = dot_nt(q2, kf) * HEAD_SIZE ** (-0.5)
                expo = jnp.where(allowed, jnp.exp(jnp.where(allowed, scores, 0.0)), 0.0)
                p = (expo * (1.0 / jnp.sum(expo, -1, keepdims=True))).astype(BF16)
                prob_ref[n, h] = p
                part = dot_nn(p, vf)
                total = part if total is None else total + part
            attn_ref[at_rows, pair * LANES : (pair + 1) * LANES] = total.astype(BF16)
        return carry

    lax.fori_loop(0, n_seq, one_sequence, 0)


def head_form(ref, at_rows, h):
    group, odd = h // (QUERY_HEADS // KEY_VALUE_HEADS), h % 2
    block = group // 2 + (2 if group % 2 != odd else 0)
    return lane_half(ref[at_rows, block * LANES : (block + 1) * LANES], odd)


def mlp_kernel(plan, first, last, place, dy_ref, gain_ref, *refs):
    if first:
        x_ref, attn_ref, wo_ref, refs = refs[0], refs[1], refs[2], refs[3:]
    else:
        mid_in, out_in, dn_in, refs = refs[0], refs[1], refs[2], refs[3:]
    n_pieces = plan.nc * plan.ny
    gates, refs = refs[:n_pieces], refs[n_pieces:]
    downs, refs = refs[:n_pieces], refs[n_pieces:]
    if last:
        out_ref, dmid_ref, dgain_ref, refs = refs[0], refs[1], refs[2], refs[3:]
    else:
        mid_ref, out_ref, dn_ref, refs = refs[0], refs[1], refs[2], refs[3:]
    gg_out, refs = refs[: plan.nc], refs[plan.nc :]
    gd_out, refs = refs[: plan.nc], refs[plan.nc :]
    (wg, wu, wd3, wd, gg, gu, gd, xs) = refs
    width, lanes = plan.width, plan.lanes
    z_at, y_at = place[2], place[3]
    rows, cols = plan.ff_rows, plan.ff_cols
    blocks = [(rc, ry, rz) for rc in range(plan.nc) for ry in range(plan.ny) for rz in range(plan.nz)]

    def spot(rc, ry, rz):
        shard = (z_at ^ rz) * plan.ny + (y_at + ry) % plan.ny
        return shard, pl.ds(pl.multiple_of(rc * cols + shard * rows, rows), rows)

    for rc, ry, rz in blocks:
        shard, at = spot(rc, ry, rz)
        piece = gates[rc * plan.ny + ry]
        wg[at, :] = piece[rz, :rows]
        wu[at, :] = piece[rz, rows:]
        wd3[shard, :, rc * cols : (rc + 1) * cols] = downs[rc * plan.ny + ry][rz]
    tokens = xs.shape[0]
    gain = gain_ref[1:2]
    xs[:, lanes - LANES :] = jnp.zeros((tokens, LANES), F32)
    if first:
        xs[:, :width] = x_ref[...].astype(F32)
        mid = xs[...] + dot_nt(attn_ref[...], wo_ref[...])
    else:
        mid = mid_in[...]
    inv = lax.rsqrt(jnp.sum(mid * mid, -1, keepdims=True) * (1.0 / width) + EPS_NORM)
    unit = mid * inv
    normed = (unit * gain).astype(BF16)
    xs[:, :width] = dy_ref[...].astype(F32)
    dy = xs[...].astype(BF16)
    gate = dot_nt(normed, wg[...])
    upper = dot_nt(normed, wu[...])
    units = plan.nc * cols
    wd[width:, :] = jnp.zeros((lanes - width, units), BF16)
    wd[:width, :] = jnp.concatenate([wd3[s].astype(F32) for s in range(plan.shards)], 0).astype(BF16)
    dhidden = dot_nn(dy, wd[...])
    sigma = 1.0 / (1.0 + jnp.exp(-gate))
    act = gate * sigma
    hid = (act * upper).astype(BF16)
    dgate = (dhidden * upper * sigma * (1.0 + gate * (1.0 - sigma))).astype(BF16)
    dupper = (dhidden * act).astype(BF16)
    gg[...] = dot_tn(dgate, normed).astype(BF16)
    gu[...] = dot_tn(dupper, normed).astype(BF16)
    down = dot_tn(dy, hid)
    for s in range(plan.shards):
        gd[s] = down[s * plan.out_rows : (s + 1) * plan.out_rows].astype(BF16)
    for rc, ry, rz in blocks:
        shard, at = spot(rc, ry, rz)
        gg_out[rc][ry, rz, :rows] = gg[at, :]
        gg_out[rc][ry, rz, rows:] = gu[at, :]
        gd_out[rc][ry, rz] = gd[shard, :, rc * cols : (rc + 1) * cols]
    out = (mid if first else out_in[...]) + dot_nt(hid, wd[...])
    dnormed = dot_nn(dgate, wg[...]) + dot_nn(dupper, wu[...])
    if not first:
        dnormed = dnormed + dn_in[...]
    if last:
        out_ref[...] = out[:, :width].astype(BF16)
        total = jnp.sum(dnormed * unit, 0, keepdims=True)
        dgain_ref[...] = jnp.broadcast_to(total, dgain_ref.shape)
        scaled = dnormed * gain
        dmid_ref[...] = (
            inv * (scaled - unit * (jnp.sum(scaled * unit, -1, keepdims=True) * (1.0 / width))) + xs[...]
        )
    else:
        mid_ref[...] = mid
        out_ref[...] = out
        dn_ref[...] = dnormed


def backward_in_kernel(dmid_ref, attn_ref, wo_ref, da_ref, grad_ref):
    dmid_b = dmid_ref[...].astype(BF16)
    da_ref[...] = dot_nn(dmid_b, wo_ref[...]).astype(BF16)
    grad_ref[...] = dot_tn(dmid_b, attn_ref[...]).astype(BF16)


def backward_rest_kernel(plan, place, x_ref, dmid_ref, dgain_ref, go_ref, da_ref, attn_ref, q_ref, k_ref, v_ref,
                         prob_ref, wq_ref, wk_ref, wv_ref, gain_ref, cos_ref, sin_ref, dx_ref, *refs):
    packs, refs = refs[: plan.nc], refs[plan.nc :]
    (dq_ref, dkv_ref, pack, xs) = refs
    width, lanes = plan.width, plan.lanes
    x_at, c_at, z_at, y_at = place[0], place[1], place[2], place[3]
    tokens = xs.shape[0]
    n_seq = tokens // SEQUENCE_LENGTH
    cos = cos_ref[...]
    sin = sin_ref[...]

    def unrotate(block):
        return block * cos - swap_halves(block) * sin

    def one_sequence(n, carry):
        at_rows = pl.ds(pl.multiple_of(n * SEQUENCE_LENGTH, SEQUENCE_LENGTH), SEQUENCE_LENGTH)
        dk = [None] * KEY_VALUE_HEADS
        dv = [None] * KEY_VALUE_HEADS
        for pair in range(lanes // LANES):
            at = slice(pair * LANES, (pair + 1) * LANES)
            q2 = q_ref[at_rows, at]
            da2 = da_ref[at_rows, at]
            prod = da2.astype(F32) * attn_ref[at_rows, at].astype(F32)
            total = None
            for odd in range(2):
                h = pair * 2 + odd
                if h >= QUERY_HEADS:
                    continue
                group = h // (QUERY_HEADS // KEY_VALUE_HEADS)
                kf = head_form(k_ref, at_rows, h)
                vf = head_form(v_ref, at_rows, h)
                p = prob_ref[n, h]
                delta = jnp.sum(lane_half(prod, odd), -1, keepdims=True)
                dp = dot_nt(da2, vf)
                ds = (p.astype(F32) * (dp - delta) * HEAD_SIZE ** (-0.5)).astype(BF16)
                part = dot_nn(ds, kf)
                total = part if total is None else total + part
                dvp = dot_tn(p, lane_half(da2, odd))
                dkp = dot_tn(ds, lane_half(q2, odd))
                dv[group] = dvp if dv[group] is None else dv[group] + dvp
                dk[group] = dkp if dk[group] is None else dk[group] + dkp
            dq_ref[at_rows, at] = unrotate(total).astype(BF16)
        for slot, (parts, turn) in enumerate(((dk, unrotate), (dv, lambda b: b))):
            whole = [g + pltpu.roll(g, HEAD_SIZE, 1) for g in parts]
            for b in range(2):
                block = lane_half(whole[2 * b], 0)
                if 2 * b + 1 < KEY_VALUE_HEADS:
                    block = block + lane_half(whole[2 * b + 1], 1)
                dkv_ref[slot, at_rows, b * LANES : (b + 1) * LANES] = turn(block).astype(BF16)
        return carry

    lax.fori_loop(0, n_seq, one_sequence, 0)
    xs[:, lanes - LANES :] = jnp.zeros((tokens, LANES), F32)
    xs[:, :width] = x_ref[...].astype(F32)
    dq, dk, dv = dq_ref[...], dkv_ref[0], dkv_ref[1]
    xfull = xs[...]
    inv = lax.rsqrt(jnp.sum(xfull * xfull, -1, keepdims=True) * (1.0 / width) + EPS_NORM)
    gain = gain_ref[0:1]
    unit = xfull * inv
    normed = (unit * gain).astype(BF16)
    dnormed = dot_nn(dq, wq_ref[...]) + dot_nn(dk, wk_ref[...]) + dot_nn(dv, wv_ref[...])
    lane = lax.broadcasted_iota(jnp.int32, (1, lanes), 1)
    dnormed = jnp.where(lane < width, dnormed, 0.0)
    dgain = jnp.sum(dnormed * unit, 0, keepdims=True)
    grad_q = dot_tn(dq, normed)
    grad_k = dot_tn(dk, normed)
    grad_v = dot_tn(dv, normed)
    grad_out = go_ref[...].astype(F32)
    at = width - (lanes - LANES)
    row = lax.broadcasted_iota(jnp.int32, (LANES, lanes), 0)
    sheet = jnp.where(row == at, dgain, 0.0) + jnp.where(row == at + 1, dgain_ref[0:1], 0.0)
    side = sheet.T
    grad_q = jnp.concatenate([grad_q[:, : lanes - LANES], grad_q[:, lanes - LANES :] + side], 1)
    rows, krows = plan.out_rows, plan.kv_rows
    for s in range(plan.shards):
        a, b = slice(s * rows, (s + 1) * rows), slice(s * krows, (s + 1) * krows)
        pack[0, s] = jnp.concatenate([grad_q[a], grad_k[b]], 0).astype(BF16)
        pack[1, s] = jnp.concatenate([grad_v[b], grad_out[a]], 0).astype(BF16)
    part_rows = plan.half_rows // plan.nx
    for rc in range(2):
        for rx in range(plan.nx):
            for ry in range(plan.ny):
                for rz in range(plan.nz):
                    shard = (z_at ^ rz) * plan.ny + (y_at + ry) % plan.ny
                    at = pl.multiple_of((x_at + rx) % plan.nx * part_rows, part_rows)
                    block = pack[(c_at + rc) % 2, shard, pl.ds(at, part_rows)]
                    if plan.nc == 2:
                        packs[rc][rx, ry, rz] = block
                    else:
                        packs[0][rc, rx, ry, rz] = block
    scaled = dnormed * gain
    dx = inv * (scaled - unit * (jnp.sum(scaled * unit, -1, keepdims=True) * (1.0 / width))) + dmid_ref[...]
    dx_ref[...] = dx[:, :width].astype(BF16)


def unpack_ff_kernel(plan, place, mine_ref, other_ref, gate_ref, up_ref):
    rows = plan.ff_rows
    for rc, ref in enumerate((mine_ref, other_ref)):
        for rx in range(plan.nx):
            part = (place[0] + rx + 1) % plan.nx * plan.nc + (place[1] + rc) % plan.nc
            at = pl.ds(pl.multiple_of(part * rows, rows), rows)
            gate_ref[at, :] = ref[rx, :rows, : plan.width].astype(F32)
            up_ref[at, :] = ref[rx, rows:, : plan.width].astype(F32)


def unpack_attention_kernel(plan, place, mine_ref, other_ref, q_ref, k_ref, v_ref, o_ref, gain_a_ref, gain_m_ref):
    width, rows, krows, lanes = plan.width, plan.out_rows, plan.kv_rows, plan.lanes
    mine = [mine_ref[i].astype(F32) for i in range(plan.nx)]
    other = [other_ref[i].astype(F32) for i in range(plan.nx)]
    swap = place[0] != 0
    mine = jnp.where(swap, jnp.concatenate(mine[::-1], 0), jnp.concatenate(mine, 0))
    other = jnp.where(swap, jnp.concatenate(other[::-1], 0), jnp.concatenate(other, 0))
    one = jnp.where(place[1] == 0, mine, other)
    two = jnp.where(place[1] == 0, other, mine)
    q_ref[...] = one[:rows, :width]
    k_ref[...] = one[rows:, :width]
    v_ref[...] = two[:krows, :width]
    o_ref[...] = two[krows:, :width]
    last = jnp.concatenate([one[:, lanes - LANES :], jnp.zeros((LANES - rows - krows, LANES), F32)], 0).T
    at = width - (lanes - LANES)
    gain_a_ref[...] = last[at : at + 1, :rows]
    gain_m_ref[...] = last[at + 1 : at + 2, :rows]


VMEM = pl.BlockSpec(memory_space=pltpu.VMEM)
SMEM = pl.BlockSpec(memory_space=pltpu.SMEM)


def shape_of(dims, kind):
    return jax.ShapeDtypeStruct(dims, kind)


def limit(plan, mib):
    return pltpu.CompilerParams(vmem_limit_bytes=(mib if plan.direct else 60) * 2**20)


def kept(plan):
    return pltpu.VMEM if plan.direct else shape_of


def cost(micros):
    return pl.CostEstimate(flops=int(micros * 1e9), transcendentals=0, bytes_accessed=int(micros * 1e6))


def attention_forward(plan, place, tokens, cos, sin, pieces):
    rows, lanes = tokens.shape[0], plan.lanes
    n_seq = rows // SEQUENCE_LENGTH
    held = kept(plan)
    return pl.pallas_call(
        functools.partial(attention_forward_kernel, plan, len(pieces)),
        name="attention_forward",
        in_specs=[SMEM] + [VMEM] * (3 + len(pieces)),
        out_specs=[VMEM] * 10,
        out_shape=[
            held((rows, lanes), BF16),
            held((rows, 4 * LANES), BF16),
            held((rows, 4 * LANES), BF16),
            held((rows, lanes), BF16),
            held((n_seq, QUERY_HEADS, SEQUENCE_LENGTH, SEQUENCE_LENGTH), BF16),
            held((lanes, lanes), BF16),
            held((2 * LANES, lanes), BF16),
            held((2 * LANES, lanes), BF16),
            held((lanes, lanes), BF16),
            held((8, lanes), F32),
        ],
        scratch_shapes=[
            pltpu.VMEM((2, plan.shards, plan.half_rows, lanes), BF16),
            pltpu.VMEM((rows, lanes), F32),
        ],
        cost_estimate=cost(10),
            compiler_params=limit(plan, 12),
    )(place, tokens, cos, sin, *pieces)


def mlp(plan, place, first, last, cotangent, gain, inputs, gates, downs):
    rows, lanes = cotangent.shape[0], plan.lanes
    held = kept(plan)
    units = plan.nc * plan.ff_cols
    ff = held((plan.ny, plan.nz, 2 * plan.ff_rows, lanes), BF16)
    dn = held((plan.ny, plan.nz, plan.out_rows, plan.ff_cols), BF16)
    whole = held((rows, lanes), F32)
    results = [shape_of((rows, plan.width), BF16), whole, held((8, lanes), F32)] if last else [whole] * 3
    return pl.pallas_call(
        functools.partial(mlp_kernel, plan, first, last),
        name="mlp",
        in_specs=[SMEM] + [VMEM] * (5 + len(gates) + len(downs)),
        out_specs=[VMEM] * (3 + 2 * plan.nc),
        out_shape=results + [ff] * plan.nc + [dn] * plan.nc,
        scratch_shapes=[
            pltpu.VMEM((units, lanes), BF16),
            pltpu.VMEM((units, lanes), BF16),
            pltpu.VMEM((plan.shards, plan.out_rows, units), BF16),
            pltpu.VMEM((lanes, units), BF16),
            pltpu.VMEM((units, lanes), BF16),
            pltpu.VMEM((units, lanes), BF16),
            pltpu.VMEM((plan.shards, plan.out_rows, units), BF16),
            pltpu.VMEM((rows, lanes), F32),
        ],
        cost_estimate=cost(12),
            compiler_params=limit(plan, 24),
    )(place, cotangent, gain, *inputs, *gates, *downs)


def attention_backward(plan, place, tokens, dmid, dgain, attn, q, k, v, prob, wq, wk, wv, wo, gain, cos, sin):
    rows, lanes = tokens.shape[0], plan.lanes
    held = kept(plan)
    da, grad_out = pl.pallas_call(
        backward_in_kernel,
        name="backward_in",
        in_specs=[VMEM] * 3,
        out_specs=[VMEM] * 2,
        out_shape=[held((rows, lanes), BF16), held((lanes, lanes), BF16)],
        cost_estimate=cost(4),
        compiler_params=limit(plan, 6),
    )(dmid, attn, wo)
    block = (plan.nx, plan.ny, plan.nz, plan.half_rows // plan.nx, lanes)
    if plan.nc == 2:
        packs = [held(block, BF16)] * 2
    else:
        packs = [shape_of((2,) + block, BF16)]
    return pl.pallas_call(
        functools.partial(backward_rest_kernel, plan),
        name="backward_rest",
        in_specs=[SMEM] + [VMEM] * 16,
        out_specs=[VMEM] * (1 + len(packs)),
        out_shape=[shape_of((rows, plan.width), BF16)] + packs,
        scratch_shapes=[
            pltpu.VMEM((rows, lanes), BF16),
            pltpu.VMEM((2, rows, 2 * LANES), BF16),
            pltpu.VMEM((2, plan.shards, plan.half_rows, lanes), BF16),
            pltpu.VMEM((rows, lanes), F32),
        ],
        cost_estimate=cost(14),
        compiler_params=limit(plan, 16),
    )(place, tokens, dmid, dgain, grad_out, da, attn, q, k, v, prob, wq, wk, wv, gain, cos, sin)


def unpack(plan, kernel, place, mine, other, shapes):
    return pl.pallas_call(
        functools.partial(kernel, plan),
        in_specs=[SMEM, VMEM, VMEM],
        out_specs=[VMEM] * len(shapes),
        out_shape=[shape_of(dims, F32) for dims in shapes],
        cost_estimate=cost(2),
        compiler_params=limit(plan, 6),
    )(place, mine, other)


def shift(plan, dim, amount):
    if dim in "xc":
        axis, outer, inner, first = "dp", plan.nx, plan.nc, dim == "x"
    else:
        axis, outer, inner, first = "fsdp", plan.nz, plan.ny, dim == "z"
    pairs = []
    for o in range(outer):
        for i in range(inner):
            if dim == "z":
                to = (o ^ amount, i)
            else:
                to = ((o + amount) % outer, i) if first else (o, (i + amount) % inner)
            pairs.append((o * inner + i, to[0] * inner + to[1]))
    return axis, pairs


def send(plan, value, dim, amount=1):
    axis, pairs = shift(plan, dim, amount)
    return lax.ppermute(value, axis, pairs)


def spread(plan, piece, dims):
    around = [piece] + [send(plan, piece, "z", k) for k in range(1, plan.nz)]
    stack = jnp.stack(around)
    held = {(0, 0, 0): stack}
    for dim in dims:
        at = "cxy".index(dim)
        for place, value in list(held.items()):
            place = list(place)
            place[at] = 1
            held[tuple(place)] = send(plan, value, dim)
    return held


def add(a, b):
    return (a.astype(F32) + b.astype(F32)).astype(BF16)


def reduce_z(plan, stack):
    got = [send(plan, stack[k], "z", k) for k in range(1, plan.nz)]
    total = stack[0].astype(F32)
    for value in got:
        total = total + value.astype(F32)
    return total.astype(BF16)


def pad_four(results, nc):
    results = list(results)
    return results if nc == 2 else results[:4] + [None, results[4], None]


def layer(plan, tokens, cotangent, w_query, w_key, w_value, w_out, w_gate, w_up, w_down, gain_attn, gain_mlp):
    cos, sin = rope_tables()
    width, lanes, hidden = plan.width, plan.lanes, plan.hidden
    d_at, s_at = lax.axis_index("dp"), lax.axis_index("fsdp")
    if plan.direct:
        x_at, c_at = d_at // plan.nc, d_at % plan.nc
        place = jnp.stack([x_at, c_at, s_at // plan.ny, s_at % plan.ny]).astype(jnp.int32)
        place, x_first, c_first, ff_at, d_at, w_query = lax.optimization_barrier(
            (place, x_at == 0, c_at == 0, d_at * plan.ff_rows, d_at, w_query)
        )
    else:
        place = jnp.zeros((4,), jnp.int32)

    def widen(rows, extra=None):
        rest = lanes - width
        if extra is None:
            return jnp.pad(rows, ((0, 0), (0, rest)))
        side = jnp.pad(extra, ((0, rows.shape[0] - extra.shape[0]), (0, rest - extra.shape[1])))
        return jnp.concatenate([rows, side], 1)

    def all_rows(w):
        return lax.all_gather(w.T, "fsdp", axis=0, tiled=True)

    if plan.direct:
        gains = jnp.stack([gain_attn, gain_mlp], 1)
        first = widen(jnp.concatenate([w_query.T, w_key.T], 0), gains)
        second = widen(jnp.concatenate([w_value.T, w_out.T], 0))
        own = jnp.where(c_first, first, second)
        part_rows = plan.half_rows // plan.nx
        own = jnp.where(x_first, own[:part_rows], own[part_rows:])
        gate_own = widen(
            jnp.concatenate(
                [lax.dynamic_slice_in_dim(w, ff_at, plan.ff_rows, 1).T for w in (w_gate, w_up)], 0
            )
        )
        down_own = w_down.reshape(plan.shards, plan.parts, plan.ff_rows, plan.out_rows)
        down_own = lax.dynamic_index_in_dim(down_own, d_at, 1, False).reshape(plan.ff_cols, plan.out_rows).T
        held_a = spread(plan, own, "yxc")
        spots = [(rc, rx, ry) for rc in range(plan.nc) for rx in range(plan.nx) for ry in range(plan.ny)]
        pieces = [held_a[spot] for spot in spots]
        held_f = spread(plan, gate_own, "xyc")
        held_d = spread(plan, down_own, "yxc")
        keys = [[(rc, rx, ry) for rc in range(plan.nc) for ry in range(plan.ny)] for rx in range(plan.nx)]
        gates = [[held_f[key] for key in part] for part in keys]
        downs = [[held_d[key] for key in part] for part in keys]
    else:
        gains = jnp.stack(
            [lax.all_gather(g, "fsdp", axis=0, tiled=True) for g in (gain_attn, gain_mlp)], 1
        )
        pieces = [
            widen(jnp.concatenate([all_rows(w_query), all_rows(w_key)], 0), gains)[None],
            widen(jnp.concatenate([all_rows(w_value), all_rows(w_out)], 0))[None],
        ]
        gates = [[widen(jnp.concatenate([all_rows(w_gate), all_rows(w_up)], 0))[None]]]
        downs = [[all_rows(w_down)[None]]]

    q, k, v, attn, prob, wq, wk, wv, wo, gain = attention_forward(plan, place, tokens, cos, sin, pieces)
    carried, grads = (tokens, attn, wo), []
    for i in range(plan.nx):
        *carried, gate_a, gate_b, down_a, down_b = pad_four(
            mlp(plan, place, i == 0, i == plan.nx - 1, cotangent, gain, carried, gates[i], downs[i]), plan.nc
        )
        grads.append(((gate_a, gate_b), (down_a, down_b)))
    output, dmid, dgain = carried
    grad_tokens, *packs = attention_backward(
        plan, place, tokens, dmid, dgain, attn, q, k, v, prob, wq, wk, wv, wo, gain, cos, sin
    )
    rows, krows = plan.out_rows, plan.kv_rows

    if plan.direct:

        def fold(pieces, dims):
            mine = [add(a, send(plan, b, "c")) for a, b in pieces]
            away, keep = mine
            if dims == "xy":
                part = add(keep, send(plan, away, "x"))
                part = add(part[0], send(plan, part[1], "y"))
            else:
                both = jnp.stack([keep[1], away[1]])
                got = send(plan, both, "y")
                there = send(plan, add(away[0], got[1]), "x")
                part = add(add(keep[0], got[0]), there)
            part = reduce_z(plan, part)
            both = jnp.stack([part, send(plan, part, "x")])
            return both, send(plan, both, "c")

        def in_order(both, other):
            quads = jnp.stack([both, other], 1)
            quads = jnp.where(c_first, quads, quads[:, ::-1])
            return jnp.where(x_first, quads[::-1], quads)

        ff_rows = plan.ff_rows
        both, other = fold([g[0] for g in grads], "xy")
        grad_gate, grad_up = unpack(plan, unpack_ff_kernel, place, both, other, [(plan.parts * ff_rows, width)] * 2)
        quads = in_order(*fold([g[1] for g in grads], "yx"))
        quads = quads.reshape(plan.parts, rows, plan.shards, ff_rows)
        grad_down = quads.transpose(1, 2, 0, 3).reshape(rows, hidden).astype(F32)
        got = send(plan, packs[1], "c")
        there = send(plan, add(packs[0][1], got[1]), "x")
        part = add(add(packs[0][0], got[0]), there)
        part = add(part[0], send(plan, part[1], "y"))
        part = reduce_z(plan, part)
        part, grad_down = lax.optimization_barrier((part, grad_down))
        there = send(plan, part, "x")
        both = jnp.stack([part, there])
        both, grad_gate, grad_up = lax.optimization_barrier((both, grad_gate, grad_up))
        other = send(plan, both, "c")
        shapes = [(rows, width), (krows, width), (krows, width), (rows, width), (1, rows), (1, rows)]
        *results, gain_a, gain_m = unpack(plan, unpack_attention_kernel, place, both, other, shapes)
        return (
            output,
            grad_tokens,
            *[result.T for result in results],
            grad_gate.T,
            grad_up.T,
            grad_down.T,
            gain_a.reshape(rows),
            gain_m.reshape(rows),
        )
    else:

        def total(value):
            part = lax.psum_scatter(value.astype(F32), "fsdp", scatter_dimension=0, tiled=True)
            return lax.psum(part, "dp")

        both = grads[0][0][0].reshape(2, hidden, lanes)[:, :, :width]
        grad_gate, grad_up = total(both[0]).T, total(both[1]).T
        grad_down = total(grads[0][1][0].reshape(width, hidden)).T
        whole = packs[0].reshape(2, width + plan.kv, lanes)
        one = jnp.concatenate([total(whole[0, :width]), total(whole[0, width:])], 0)
        two = jnp.concatenate([total(whole[1, : plan.kv]), total(whole[1, plan.kv :])], 0)
        rows, krows = width // plan.fsdp, plan.kv // plan.fsdp
    return (
        output,
        grad_tokens,
        one[:rows, :width].T,
        one[rows:, :width].T,
        two[:krows, :width].T,
        two[krows:, :width].T,
        grad_gate,
        grad_up,
        grad_down,
        one[:rows, width],
        one[:rows, width + 1],
    )


def solution(mesh):
    rows = P(("dp", "fsdp"), None)
    cols = P(None, "fsdp")
    one = P("fsdp")

    def run(*args):
        plan = Plan(mesh, args[0].shape[1], args[8].shape[0])
        step = jax.shard_map(
            functools.partial(layer, plan),
            mesh=mesh,
            in_specs=(rows, rows) + (cols,) * 7 + (one, one),
            out_specs=(rows, rows) + (cols,) * 7 + (one, one),
            check_vma=False,
        )
        return step(*args)

    return run
```

```python
import functools

import jax
import jax.numpy as jnp
import numpy as np
from jax import lax
from jax.experimental import pallas as pl
from jax.experimental.pallas import tpu as pltpu
from jax.sharding import PartitionSpec as P


QUERY_HEADS = 9
KEY_VALUE_HEADS = 3
HEAD_SIZE = 64
SEQUENCE_LENGTH = 192

EPS_NORM = 1e-05
ROPE_BASE = 100000.0


F32 = jnp.float32
BF16 = jnp.bfloat16
LANES = 128


def up_to(value, step):
    return -(-value // step) * step


def dot_nn(left, right):
    return lax.dot_general(left, right, (((1,), (0,)), ((), ())), preferred_element_type=F32)


def dot_nt(left, right):
    return lax.dot_general(left, right, (((1,), (1,)), ((), ())), preferred_element_type=F32)


def dot_tn(left, right):
    return lax.dot_general(left, right, (((0,), (0,)), ((), ())), preferred_element_type=F32)


def rope_tables():
    half = HEAD_SIZE // 2
    position = np.arange(SEQUENCE_LENGTH).astype(np.float32)
    freqs = np.power(
        np.float32(ROPE_BASE), -(np.arange(half).astype(np.float32) * np.float32(2.0 / HEAD_SIZE))
    ).astype(np.float32)
    angles = (position[:, None] * freqs[None, :]).astype(np.float32)
    cosine = np.cos(angles.astype(np.float64)).astype(np.float32)
    sine = np.sin(angles.astype(np.float64)).astype(np.float32)
    reps = LANES // HEAD_SIZE
    return (
        jnp.asarray(np.concatenate([cosine, cosine] * reps, 1)),
        jnp.asarray(np.concatenate([-sine, sine] * reps, 1)),
    )


def swap_halves(block):
    half = HEAD_SIZE // 2
    lane = lax.broadcasted_iota(jnp.int32, block.shape, block.ndim - 1)
    return jnp.where(
        lane % HEAD_SIZE < half,
        pltpu.roll(block, LANES - half, block.ndim - 1),
        pltpu.roll(block, half, block.ndim - 1),
    )


def lane_half(block, odd):
    lane = lax.broadcasted_iota(jnp.int32, block.shape, block.ndim - 1)
    keep = (lane >= HEAD_SIZE) if odd else (lane < HEAD_SIZE)
    return jnp.where(keep, block, jnp.zeros_like(block))


class Plan:
    def __init__(self, mesh, width, hidden):
        self.dp, self.fsdp = mesh.shape["dp"], mesh.shape["fsdp"]
        self.width, self.hidden = width, hidden
        self.kv = KEY_VALUE_HEADS * HEAD_SIZE
        self.lanes = up_to(width, LANES)
        self.main = self.lanes - LANES
        assert width - self.main == HEAD_SIZE and 2 * HEAD_SIZE == LANES
        self.nx, self.nc = self.dp // 2, 2
        self.nz, self.ny = self.fsdp // 2, 2
        s, d = self.fsdp, self.dp
        self.direct = (
            d == 4
            and s == 8
            and (width // s) % 8 == 0
            and (self.kv // s) % 8 == 0
            and ((width + self.kv) // s) % (16 * (d // 2)) == 0
            and (hidden // s // d) % 16 == 0
            and (hidden // d) % LANES == 0
        )
        if not self.direct:
            self.nx = self.nc = self.nz = self.ny = 1
        self.shards = self.nz * self.ny
        self.parts = self.nx * self.nc
        self.out_rows = width // self.shards
        self.kv_rows = self.kv // self.shards
        self.half_rows = self.out_rows + self.kv_rows
        self.ff_rows = hidden // self.shards // self.parts
        self.ff_cols = hidden // self.parts

    def key(self):
        return (self.dp, self.fsdp, self.width, self.hidden)


def attention_forward_kernel(plan, n_pieces, place, x_ref, cos_ref, sin_ref, *refs):
    pieces, refs = refs[:n_pieces], refs[n_pieces:]
    (q_ref, k_ref, v_ref, attn_ref, prob_ref, wq_ref, wk_ref, wv_ref, wo_ref, gain_ref, pack, xs) = refs
    width, lanes, kv = plan.width, plan.lanes, plan.kv
    x_at, c_at, z_at, y_at = place[0], place[1], place[2], place[3]
    part_rows = plan.half_rows // plan.nx
    spots = [(rc, rx, ry) for rc in range(2) for rx in range(plan.nx) for ry in range(plan.ny)]
    for (rc, rx, ry), piece in zip(spots, pieces):
        half = (c_at + rc) % 2
        at = pl.multiple_of((x_at + rx) % plan.nx * part_rows, part_rows)
        for k in range(plan.nz):
            shard = (z_at ^ k) * plan.ny + (y_at + ry) % plan.ny
            pack[half, shard, pl.ds(at, part_rows)] = piece[k]
    xs[:, lanes - LANES :] = jnp.zeros((xs.shape[0], LANES), F32)
    xs[:, :width] = x_ref[...].astype(F32)
    xfull = xs[...]
    inv = lax.rsqrt(jnp.sum(xfull * xfull, -1, keepdims=True) * (1.0 / width) + EPS_NORM)
    rows, krows = plan.out_rows, plan.kv_rows
    qs, ks, vs, os = [], [], [], []
    for s in range(plan.shards):
        first = pack[0, s].astype(F32)
        second = pack[1, s].astype(F32)
        qs.append(first[:rows])
        ks.append(first[rows:])
        vs.append(second[:krows])
        os.append(second[krows:])
    tail = jnp.zeros((lanes - width, lanes), F32)
    wq_full = jnp.concatenate(qs + [tail], 0)
    lane = lax.broadcasted_iota(jnp.int32, (lanes, lanes), 1)
    wq_ref[...] = jnp.where(lane < width, wq_full, 0.0).astype(BF16)
    kv_pad = 2 * LANES
    ktail = jnp.zeros((kv_pad - kv, lanes), F32)
    wk_ref[...] = jnp.concatenate(ks + [ktail], 0).astype(BF16)
    wv_ref[...] = jnp.concatenate(vs + [ktail], 0).astype(BF16)
    wo_ref[...] = jnp.concatenate(os + [tail], 0).astype(BF16)
    turned = wq_full[:, lanes - LANES :].T
    at = width - (lanes - LANES)
    gain_ref[...] = turned[at : at + 8]
    gain = turned[at : at + 1]
    normed = (xfull * inv * gain).astype(BF16)
    tokens = xs.shape[0]
    n_seq = tokens // SEQUENCE_LENGTH
    cos = cos_ref[...][None]
    sin = sin_ref[...][None]

    def rotate(block):
        cube = block.reshape(n_seq, SEQUENCE_LENGTH, LANES)
        return (cube * cos + swap_halves(cube) * sin).reshape(tokens, LANES)

    q = dot_nt(normed, wq_ref[...])
    for b in range(lanes // LANES):
        q_ref[:, b * LANES : (b + 1) * LANES] = rotate(q[:, b * LANES : (b + 1) * LANES]).astype(BF16)
    k = dot_nt(normed, wk_ref[...])
    v = dot_nt(normed, wv_ref[...])
    for b in range(2):
        kb = rotate(k[:, b * LANES : (b + 1) * LANES])
        vb = v[:, b * LANES : (b + 1) * LANES]
        k_ref[:, b * LANES : (b + 1) * LANES] = kb.astype(BF16)
        v_ref[:, b * LANES : (b + 1) * LANES] = vb.astype(BF16)
        k_ref[:, (b + 2) * LANES : (b + 3) * LANES] = pltpu.roll(kb, HEAD_SIZE, 1).astype(BF16)
        v_ref[:, (b + 2) * LANES : (b + 3) * LANES] = pltpu.roll(vb, HEAD_SIZE, 1).astype(BF16)

    shape = (SEQUENCE_LENGTH, SEQUENCE_LENGTH)
    allowed = lax.broadcasted_iota(jnp.int32, shape, 0) >= lax.broadcasted_iota(jnp.int32, shape, 1)

    def one_sequence(n, carry):
        at_rows = pl.ds(pl.multiple_of(n * SEQUENCE_LENGTH, SEQUENCE_LENGTH), SEQUENCE_LENGTH)
        for pair in range(lanes // LANES):
            q2 = q_ref[at_rows, pair * LANES : (pair + 1) * LANES]
            total = None
            for odd in range(2):
                h = pair * 2 + odd
                if h >= QUERY_HEADS:
                    continue
                kf = head_form(k_ref, at_rows, h)
                vf = head_form(v_ref, at_rows, h)
                scores = dot_nt(q2, kf) * HEAD_SIZE ** (-0.5)
                expo = jnp.where(allowed, jnp.exp(jnp.where(allowed, scores, 0.0)), 0.0)
                p = (expo * (1.0 / jnp.sum(expo, -1, keepdims=True))).astype(BF16)
                prob_ref[n, h] = p
                part = dot_nn(p, vf)
                total = part if total is None else total + part
            attn_ref[at_rows, pair * LANES : (pair + 1) * LANES] = total.astype(BF16)
        return carry

    lax.fori_loop(0, n_seq, one_sequence, 0)


def head_form(ref, at_rows, h):
    group, odd = h // (QUERY_HEADS // KEY_VALUE_HEADS), h % 2
    block = group // 2 + (2 if group % 2 != odd else 0)
    return lane_half(ref[at_rows, block * LANES : (block + 1) * LANES], odd)


def mlp_kernel(plan, first, last, place, dy_ref, gain_ref, *refs):
    if first:
        x_ref, attn_ref, wo_ref, refs = refs[0], refs[1], refs[2], refs[3:]
    else:
        mid_in, out_in, dn_in, refs = refs[0], refs[1], refs[2], refs[3:]
    n_pieces = plan.nc * plan.ny
    gates, refs = refs[:n_pieces], refs[n_pieces:]
    downs, refs = refs[:n_pieces], refs[n_pieces:]
    if last:
        out_ref, dmid_ref, dgain_ref, refs = refs[0], refs[1], refs[2], refs[3:]
    else:
        mid_ref, out_ref, dn_ref, refs = refs[0], refs[1], refs[2], refs[3:]
    gg_out, refs = refs[: plan.nc], refs[plan.nc :]
    gd_out, refs = refs[: plan.nc], refs[plan.nc :]
    (wg, wu, wd3, wd, gg, gd, xs) = refs
    width, lanes = plan.width, plan.lanes
    z_at, y_at = place[2], place[3]
    rows, cols = plan.ff_rows, plan.ff_cols
    main = plan.main
    blocks = [(rc, ry, rz) for rc in range(plan.nc) for ry in range(plan.ny) for rz in range(plan.nz)]

    def spot(rc, ry, rz):
        shard = (z_at ^ rz) * plan.ny + (y_at + ry) % plan.ny
        return shard, pl.ds(pl.multiple_of(rc * cols + shard * rows, rows), rows)

    for rc, ry, rz in blocks:
        shard, at = spot(rc, ry, rz)
        piece = gates[rc * plan.ny + ry]
        wg[at, :main] = piece[rz, :, :main]
        wu[at, :main] = piece[rz, :, main : 2 * main]
        wg[at, main:] = piece[rz, :, 2 * main :]
        wu[at, main:] = piece[rz, :, 2 * main :]
        wd3[shard, :, rc * cols : (rc + 1) * cols] = downs[rc * plan.ny + ry][rz]
    tokens = xs.shape[0]
    gain = gain_ref[1:2]
    xs[:, lanes - LANES :] = jnp.zeros((tokens, LANES), F32)
    if first:
        xs[:, :width] = x_ref[...].astype(F32)
        mid = xs[...] + dot_nt(attn_ref[...], wo_ref[...])
    else:
        mid = mid_in[...]
    inv = lax.rsqrt(jnp.sum(mid * mid, -1, keepdims=True) * (1.0 / width) + EPS_NORM)
    unit = mid * inv
    scaled = unit * gain
    normed = scaled.astype(BF16)
    turned = pltpu.roll(scaled[:, main:], HEAD_SIZE, 1).astype(BF16)
    normed_up = jnp.concatenate([normed[:, :main], turned], 1)
    xs[:, :width] = dy_ref[...].astype(F32)
    dy = xs[...].astype(BF16)
    gate = dot_nt(normed, wg[...])
    upper = dot_nt(normed_up, wu[...])
    units = plan.nc * cols
    wd[width:, :] = jnp.zeros((lanes - width, units), BF16)
    wd[:width, :] = jnp.concatenate([wd3[s].astype(F32) for s in range(plan.shards)], 0).astype(BF16)
    dhidden = dot_nn(dy, wd[...])
    sigma = 1.0 / (1.0 + jnp.exp(-gate))
    act = gate * sigma
    hid = (act * upper).astype(BF16)
    dgate = (dhidden * upper * sigma * (1.0 + gate * (1.0 - sigma))).astype(BF16)
    dupper = (dhidden * act).astype(BF16)
    grad_gate = dot_tn(dgate, normed)
    grad_up = dot_tn(dupper, normed_up)
    gg[:, :main] = grad_gate[:, :main].astype(BF16)
    gg[:, main : 2 * main] = grad_up[:, :main].astype(BF16)
    gg[:, 2 * main :] = (grad_gate[:, main:] + grad_up[:, main:]).astype(BF16)
    down = dot_tn(dy, hid)
    for s in range(plan.shards):
        gd[s] = down[s * plan.out_rows : (s + 1) * plan.out_rows].astype(BF16)
    for rc, ry, rz in blocks:
        shard, at = spot(rc, ry, rz)
        gg_out[rc][ry, rz] = gg[at, :]
        gd_out[rc][ry, rz] = gd[shard, :, rc * cols : (rc + 1) * cols]
    out = (mid if first else out_in[...]) + dot_nt(hid, wd[...])
    by_gate = dot_nn(dgate, wg[...])
    by_up = dot_nn(dupper, wu[...])
    tail = lane_half(by_gate[:, main:], 0) + pltpu.roll(lane_half(by_up[:, main:], 1), HEAD_SIZE, 1)
    dnormed = jnp.concatenate([by_gate[:, :main] + by_up[:, :main], tail], 1)
    if not first:
        dnormed = dnormed + dn_in[...]
    if last:
        out_ref[...] = out[:, :width].astype(BF16)
        total = jnp.sum(dnormed * unit, 0, keepdims=True)
        dgain_ref[...] = jnp.broadcast_to(total, dgain_ref.shape)
        scaled = dnormed * gain
        dmid_ref[...] = (
            inv * (scaled - unit * (jnp.sum(scaled * unit, -1, keepdims=True) * (1.0 / width))) + xs[...]
        )
    else:
        mid_ref[...] = mid
        out_ref[...] = out
        dn_ref[...] = dnormed


def backward_in_kernel(dmid_ref, attn_ref, wo_ref, da_ref, grad_ref):
    dmid_b = dmid_ref[...].astype(BF16)
    da_ref[...] = dot_nn(dmid_b, wo_ref[...]).astype(BF16)
    grad_ref[...] = dot_tn(dmid_b, attn_ref[...]).astype(BF16)


def backward_attention_kernel(plan, da_ref, attn_ref, q_ref, k_ref, v_ref, prob_ref, cos_ref, sin_ref, dq_ref, dkv_ref):
    lanes = plan.lanes
    n_seq = q_ref.shape[0] // SEQUENCE_LENGTH
    cos = cos_ref[...]
    sin = sin_ref[...]

    def unrotate(block):
        return block * cos - swap_halves(block) * sin

    def one_sequence(n, carry):
        at_rows = pl.ds(pl.multiple_of(n * SEQUENCE_LENGTH, SEQUENCE_LENGTH), SEQUENCE_LENGTH)
        dk = [None] * KEY_VALUE_HEADS
        dv = [None] * KEY_VALUE_HEADS
        for pair in range(lanes // LANES):
            at = slice(pair * LANES, (pair + 1) * LANES)
            q2 = q_ref[at_rows, at]
            da2 = da_ref[at_rows, at]
            prod = da2.astype(F32) * attn_ref[at_rows, at].astype(F32)
            total = None
            for odd in range(2):
                h = pair * 2 + odd
                if h >= QUERY_HEADS:
                    continue
                group = h // (QUERY_HEADS // KEY_VALUE_HEADS)
                kf = head_form(k_ref, at_rows, h)
                vf = head_form(v_ref, at_rows, h)
                p = prob_ref[n, h]
                delta = jnp.sum(lane_half(prod, odd), -1, keepdims=True)
                dp = dot_nt(da2, vf)
                ds = (p.astype(F32) * (dp - delta) * HEAD_SIZE ** (-0.5)).astype(BF16)
                part = dot_nn(ds, kf)
                total = part if total is None else total + part
                dvp = dot_tn(p, lane_half(da2, odd))
                dkp = dot_tn(ds, lane_half(q2, odd))
                dv[group] = dvp if dv[group] is None else dv[group] + dvp
                dk[group] = dkp if dk[group] is None else dk[group] + dkp
            dq_ref[at_rows, at] = unrotate(total).astype(BF16)
        for slot, (parts, turn) in enumerate(((dk, unrotate), (dv, lambda b: b))):
            whole = [g + pltpu.roll(g, HEAD_SIZE, 1) for g in parts]
            for b in range(2):
                block = lane_half(whole[2 * b], 0)
                if 2 * b + 1 < KEY_VALUE_HEADS:
                    block = block + lane_half(whole[2 * b + 1], 1)
                dkv_ref[slot, at_rows, b * LANES : (b + 1) * LANES] = turn(block).astype(BF16)
        return carry

    lax.fori_loop(0, n_seq, one_sequence, 0)


def backward_out_kernel(plan, place, x_ref, dmid_ref, dgain_ref, go_ref, dq_ref, dkv_ref, wq_ref, wk_ref, wv_ref,
                        gain_ref, dx_ref, *refs):
    packs, refs = refs[: plan.nc], refs[plan.nc :]
    (pack, xs) = refs
    width, lanes = plan.width, plan.lanes
    x_at, c_at, z_at, y_at = place[0], place[1], place[2], place[3]
    tokens = xs.shape[0]
    xs[:, lanes - LANES :] = jnp.zeros((tokens, LANES), F32)
    xs[:, :width] = x_ref[...].astype(F32)
    dq, dk, dv = dq_ref[...], dkv_ref[0], dkv_ref[1]
    xfull = xs[...]
    inv = lax.rsqrt(jnp.sum(xfull * xfull, -1, keepdims=True) * (1.0 / width) + EPS_NORM)
    gain = gain_ref[0:1]
    unit = xfull * inv
    normed = (unit * gain).astype(BF16)
    dnormed = dot_nn(dq, wq_ref[...]) + dot_nn(dk, wk_ref[...]) + dot_nn(dv, wv_ref[...])
    lane = lax.broadcasted_iota(jnp.int32, (1, lanes), 1)
    dnormed = jnp.where(lane < width, dnormed, 0.0)
    dgain = jnp.sum(dnormed * unit, 0, keepdims=True)
    grad_q = dot_tn(dq, normed)
    grad_k = dot_tn(dk, normed)
    grad_v = dot_tn(dv, normed)
    grad_out = go_ref[...].astype(F32)
    at = width - (lanes - LANES)
    row = lax.broadcasted_iota(jnp.int32, (LANES, lanes), 0)
    sheet = jnp.where(row == at, dgain, 0.0) + jnp.where(row == at + 1, dgain_ref[0:1], 0.0)
    side = sheet.T
    grad_q = jnp.concatenate([grad_q[:, : lanes - LANES], grad_q[:, lanes - LANES :] + side], 1)
    rows, krows = plan.out_rows, plan.kv_rows
    for s in range(plan.shards):
        a, b = slice(s * rows, (s + 1) * rows), slice(s * krows, (s + 1) * krows)
        pack[0, s] = jnp.concatenate([grad_q[a], grad_k[b]], 0).astype(BF16)
        pack[1, s] = jnp.concatenate([grad_v[b], grad_out[a]], 0).astype(BF16)
    part_rows = plan.half_rows // plan.nx
    for rc in range(2):
        for rx in range(plan.nx):
            for ry in range(plan.ny):
                for rz in range(plan.nz):
                    shard = (z_at ^ rz) * plan.ny + (y_at + ry) % plan.ny
                    at = pl.multiple_of((x_at + rx) % plan.nx * part_rows, part_rows)
                    block = pack[(c_at + rc) % 2, shard, pl.ds(at, part_rows)]
                    if plan.nc == 2:
                        packs[rc][rx, ry, rz] = block
                    else:
                        packs[0][rc, rx, ry, rz] = block
    scaled = dnormed * gain
    dx = inv * (scaled - unit * (jnp.sum(scaled * unit, -1, keepdims=True) * (1.0 / width))) + dmid_ref[...]
    dx_ref[...] = dx[:, :width].astype(BF16)


def unpack_ff_kernel(plan, place, mine_ref, other_ref, gate_ref, up_ref):
    rows = plan.ff_rows
    for rc, ref in enumerate((mine_ref, other_ref)):
        for rx in range(plan.nx):
            part = (place[0] + rx + 1) % plan.nx * plan.nc + (place[1] + rc) % plan.nc
            at = pl.ds(pl.multiple_of(part * rows, rows), rows)
            main = plan.main
            tail = ref[rx, :, 2 * main :].astype(F32)
            gate_ref[at, :main] = ref[rx, :, :main].astype(F32)
            gate_ref[at, main:] = tail[:, :HEAD_SIZE]
            up_ref[at, :main] = ref[rx, :, main : 2 * main].astype(F32)
            up_ref[at, main:] = pltpu.roll(tail, HEAD_SIZE, 1)[:, :HEAD_SIZE]


def unpack_attention_kernel(plan, place, mine_ref, other_ref, q_ref, k_ref, v_ref, o_ref, gain_a_ref, gain_m_ref):
    width, rows, krows, lanes = plan.width, plan.out_rows, plan.kv_rows, plan.lanes
    mine = [mine_ref[i].astype(F32) for i in range(plan.nx)]
    other = [other_ref[i].astype(F32) for i in range(plan.nx)]
    swap = place[0] != 0
    mine = jnp.where(swap, jnp.concatenate(mine[::-1], 0), jnp.concatenate(mine, 0))
    other = jnp.where(swap, jnp.concatenate(other[::-1], 0), jnp.concatenate(other, 0))
    one = jnp.where(place[1] == 0, mine, other)
    two = jnp.where(place[1] == 0, other, mine)
    q_ref[...] = one[:rows, :width]
    k_ref[...] = one[rows:, :width]
    v_ref[...] = two[:krows, :width]
    o_ref[...] = two[krows:, :width]
    last = jnp.concatenate([one[:, lanes - LANES :], jnp.zeros((LANES - rows - krows, LANES), F32)], 0).T
    at = width - (lanes - LANES)
    gain_a_ref[...] = last[at : at + 1, :rows]
    gain_m_ref[...] = last[at + 1 : at + 2, :rows]


VMEM = pl.BlockSpec(memory_space=pltpu.VMEM)
SMEM = pl.BlockSpec(memory_space=pltpu.SMEM)


def shape_of(dims, kind):
    return jax.ShapeDtypeStruct(dims, kind)


def limit(plan, mib):
    return pltpu.CompilerParams(vmem_limit_bytes=(mib if plan.direct else 60) * 2**20)


def kept(plan):
    return pltpu.VMEM if plan.direct else shape_of


def cost(micros):
    return pl.CostEstimate(flops=int(micros * 1e9), transcendentals=0, bytes_accessed=int(micros * 1e6))


def attention_forward(plan, place, tokens, cos, sin, pieces):
    rows, lanes = tokens.shape[0], plan.lanes
    n_seq = rows // SEQUENCE_LENGTH
    held = kept(plan)
    return pl.pallas_call(
        functools.partial(attention_forward_kernel, plan, len(pieces)),
        name="attention_forward",
        in_specs=[SMEM] + [VMEM] * (3 + len(pieces)),
        out_specs=[VMEM] * 10,
        out_shape=[
            held((rows, lanes), BF16),
            held((rows, 4 * LANES), BF16),
            held((rows, 4 * LANES), BF16),
            held((rows, lanes), BF16),
            held((n_seq, QUERY_HEADS, SEQUENCE_LENGTH, SEQUENCE_LENGTH), BF16),
            held((lanes, lanes), BF16),
            held((2 * LANES, lanes), BF16),
            held((2 * LANES, lanes), BF16),
            held((lanes, lanes), BF16),
            held((8, lanes), F32),
        ],
        scratch_shapes=[
            pltpu.VMEM((2, plan.shards, plan.half_rows, lanes), BF16),
            pltpu.VMEM((rows, lanes), F32),
        ],
        cost_estimate=cost(10),
            compiler_params=limit(plan, 12),
    )(place, tokens, cos, sin, *pieces)


def mlp(plan, place, first, last, cotangent, gain, inputs, gates, downs):
    rows, lanes = cotangent.shape[0], plan.lanes
    held = kept(plan)
    units = plan.nc * plan.ff_cols
    ff = held((plan.ny, plan.nz, plan.ff_rows, 2 * plan.width), BF16)
    dn = held((plan.ny, plan.nz, plan.out_rows, plan.ff_cols), BF16)
    whole = held((rows, lanes), F32)
    results = [shape_of((rows, plan.width), BF16), whole, held((8, lanes), F32)] if last else [whole] * 3
    return pl.pallas_call(
        functools.partial(mlp_kernel, plan, first, last),
        name="mlp",
        in_specs=[SMEM] + [VMEM] * (5 + len(gates) + len(downs)),
        out_specs=[VMEM] * (3 + 2 * plan.nc),
        out_shape=results + [ff] * plan.nc + [dn] * plan.nc,
        scratch_shapes=[
            pltpu.VMEM((units, lanes), BF16),
            pltpu.VMEM((units, lanes), BF16),
            pltpu.VMEM((plan.shards, plan.out_rows, units), BF16),
            pltpu.VMEM((lanes, units), BF16),
            pltpu.VMEM((units, 2 * plan.width), BF16),
            pltpu.VMEM((plan.shards, plan.out_rows, units), BF16),
            pltpu.VMEM((rows, lanes), F32),
        ],
        cost_estimate=cost(12),
            compiler_params=limit(plan, 24),
    )(place, cotangent, gain, *inputs, *gates, *downs)


def attention_backward(plan, place, tokens, dmid, dgain, attn, q, k, v, prob, wq, wk, wv, wo, gain, cos, sin):
    rows, lanes = tokens.shape[0], plan.lanes
    held = kept(plan)
    da, grad_out = pl.pallas_call(
        backward_in_kernel,
        name="backward_in",
        in_specs=[VMEM] * 3,
        out_specs=[VMEM] * 2,
        out_shape=[held((rows, lanes), BF16), held((lanes, lanes), BF16)],
        cost_estimate=cost(4),
        compiler_params=limit(plan, 6),
    )(dmid, attn, wo)
    block = (plan.nx, plan.ny, plan.nz, plan.half_rows // plan.nx, lanes)
    if plan.nc == 2:
        packs = [held(block, BF16)] * 2
    else:
        packs = [shape_of((2,) + block, BF16)]
    dq, dkv = pl.pallas_call(
        functools.partial(backward_attention_kernel, plan),
        name="backward_attention",
        in_specs=[VMEM] * 8,
        out_specs=[VMEM] * 2,
        out_shape=[held((rows, lanes), BF16), held((2, rows, 2 * LANES), BF16)],
        cost_estimate=cost(7),
        compiler_params=limit(plan, 12),
    )(da, attn, q, k, v, prob, cos, sin)
    return pl.pallas_call(
        functools.partial(backward_out_kernel, plan),
        name="backward_out",
        in_specs=[SMEM] + [VMEM] * 10,
        out_specs=[VMEM] * (1 + len(packs)),
        out_shape=[shape_of((rows, plan.width), BF16)] + packs,
        scratch_shapes=[
            pltpu.VMEM((2, plan.shards, plan.half_rows, lanes), BF16),
            pltpu.VMEM((rows, lanes), F32),
        ],
        cost_estimate=cost(4),
        compiler_params=limit(plan, 16),
    )(place, tokens, dmid, dgain, grad_out, dq, dkv, wq, wk, wv, gain)


def unpack(plan, kernel, place, mine, other, shapes):
    return pl.pallas_call(
        functools.partial(kernel, plan),
        in_specs=[SMEM, VMEM, VMEM],
        out_specs=[VMEM] * len(shapes),
        out_shape=[shape_of(dims, F32) for dims in shapes],
        cost_estimate=cost(2),
        compiler_params=limit(plan, 6),
    )(place, mine, other)


def shift(plan, dim, amount):
    if dim in "xc":
        axis, outer, inner, first = "dp", plan.nx, plan.nc, dim == "x"
    else:
        axis, outer, inner, first = "fsdp", plan.nz, plan.ny, dim == "z"
    pairs = []
    for o in range(outer):
        for i in range(inner):
            if dim == "z":
                to = (o ^ amount, i)
            else:
                to = ((o + amount) % outer, i) if first else (o, (i + amount) % inner)
            pairs.append((o * inner + i, to[0] * inner + to[1]))
    return axis, pairs


def send(plan, value, dim, amount=1):
    axis, pairs = shift(plan, dim, amount)
    return lax.ppermute(value, axis, pairs)


def spread(plan, piece, dims):
    around = [piece] + [send(plan, piece, "z", k) for k in range(1, plan.nz)]
    stack = jnp.stack(around)
    held = {(0, 0, 0): stack}
    for dim in dims:
        at = "cxy".index(dim)
        for place, value in list(held.items()):
            place = list(place)
            place[at] = 1
            held[tuple(place)] = send(plan, value, dim)
    return held


def add(a, b):
    return (a.astype(F32) + b.astype(F32)).astype(BF16)


def reduce_z(plan, stack):
    got = [send(plan, stack[k], "z", k) for k in range(1, plan.nz)]
    total = stack[0].astype(F32)
    for value in got:
        total = total + value.astype(F32)
    return total.astype(BF16)


def pad_four(results, nc):
    results = list(results)
    return results if nc == 2 else results[:4] + [None, results[4], None]


def layer(plan, tokens, cotangent, w_query, w_key, w_value, w_out, w_gate, w_up, w_down, gain_attn, gain_mlp):
    cos, sin = rope_tables()
    width, lanes, hidden = plan.width, plan.lanes, plan.hidden
    d_at, s_at = lax.axis_index("dp"), lax.axis_index("fsdp")
    if plan.direct:
        x_at, c_at = d_at // plan.nc, d_at % plan.nc
        place = jnp.stack([x_at, c_at, s_at // plan.ny, s_at % plan.ny]).astype(jnp.int32)
        place, x_first, c_first, ff_at, d_at, w_query = lax.optimization_barrier(
            (place, x_at == 0, c_at == 0, d_at * plan.ff_rows, d_at, w_query)
        )
    else:
        place = jnp.zeros((4,), jnp.int32)

    def widen(rows, extra=None):
        rest = lanes - width
        if extra is None:
            return jnp.pad(rows, ((0, 0), (0, rest)))
        side = jnp.pad(extra, ((0, rows.shape[0] - extra.shape[0]), (0, rest - extra.shape[1])))
        return jnp.concatenate([rows, side], 1)

    def abreast(gate, up):
        main = plan.main
        return jnp.concatenate([gate[:, :main], up[:, :main], gate[:, main:], up[:, main:]], 1)

    def all_rows(w):
        return lax.all_gather(w.T, "fsdp", axis=0, tiled=True)

    if plan.direct:
        gains = jnp.stack([gain_attn, gain_mlp], 1)
        first = widen(jnp.concatenate([w_query.T, w_key.T], 0), gains)
        second = widen(jnp.concatenate([w_value.T, w_out.T], 0))
        own = jnp.where(c_first, first, second)
        part_rows = plan.half_rows // plan.nx
        own = jnp.where(x_first, own[:part_rows], own[part_rows:])
        gate_own = abreast(*[lax.dynamic_slice_in_dim(w, ff_at, plan.ff_rows, 1).T for w in (w_gate, w_up)])
        down_own = w_down.reshape(plan.shards, plan.parts, plan.ff_rows, plan.out_rows)
        down_own = lax.dynamic_index_in_dim(down_own, d_at, 1, False).reshape(plan.ff_cols, plan.out_rows).T
        held_a = spread(plan, own, "yxc")
        spots = [(rc, rx, ry) for rc in range(plan.nc) for rx in range(plan.nx) for ry in range(plan.ny)]
        pieces = [held_a[spot] for spot in spots]
        held_f = spread(plan, gate_own, "xyc")
        held_d = spread(plan, down_own, "yxc")
        keys = [[(rc, rx, ry) for rc in range(plan.nc) for ry in range(plan.ny)] for rx in range(plan.nx)]
        gates = [[held_f[key] for key in part] for part in keys]
        downs = [[held_d[key] for key in part] for part in keys]
    else:
        gains = jnp.stack(
            [lax.all_gather(g, "fsdp", axis=0, tiled=True) for g in (gain_attn, gain_mlp)], 1
        )
        pieces = [
            widen(jnp.concatenate([all_rows(w_query), all_rows(w_key)], 0), gains)[None],
            widen(jnp.concatenate([all_rows(w_value), all_rows(w_out)], 0))[None],
        ]
        gates = [[abreast(all_rows(w_gate), all_rows(w_up))[None]]]
        downs = [[all_rows(w_down)[None]]]

    q, k, v, attn, prob, wq, wk, wv, wo, gain = attention_forward(plan, place, tokens, cos, sin, pieces)
    carried, grads = (tokens, attn, wo), []
    for i in range(plan.nx):
        *carried, gate_a, gate_b, down_a, down_b = pad_four(
            mlp(plan, place, i == 0, i == plan.nx - 1, cotangent, gain, carried, gates[i], downs[i]), plan.nc
        )
        grads.append(((gate_a, gate_b), (down_a, down_b)))
    output, dmid, dgain = carried
    grad_tokens, *packs = attention_backward(
        plan, place, tokens, dmid, dgain, attn, q, k, v, prob, wq, wk, wv, wo, gain, cos, sin
    )
    rows, krows = plan.out_rows, plan.kv_rows

    if plan.direct:

        def fold(pieces, dims):
            mine = [add(a, send(plan, b, "c")) for a, b in pieces]
            away, keep = mine
            if dims == "xy":
                part = add(keep, send(plan, away, "x"))
                there = send(plan, part[1], "y")
                part = add(part[0], there)
            else:
                both = jnp.stack([keep[1], away[1]])
                got = send(plan, both, "y")
                there = send(plan, add(away[0], got[1]), "x")
                part = add(add(keep[0], got[0]), there)
            part = reduce_z(plan, part)
            there = send(plan, part, "x")
            both = jnp.stack([part, there])
            return both, send(plan, both, "c")

        def in_order(both, other):
            quads = jnp.stack([both, other], 1)
            quads = jnp.where(c_first, quads, quads[:, ::-1])
            return jnp.where(x_first, quads[::-1], quads)

        ff_rows = plan.ff_rows
        both, other = fold([g[0] for g in grads], "xy")
        grad_gate, grad_up = unpack(plan, unpack_ff_kernel, place, both, other, [(plan.parts * ff_rows, width)] * 2)
        quads = in_order(*fold([g[1] for g in grads], "xy"))
        quads = quads.reshape(plan.parts, rows, plan.shards, ff_rows)
        grad_down = quads.transpose(1, 2, 0, 3).reshape(rows, hidden).astype(F32)
        got = send(plan, packs[1], "c")
        there = send(plan, add(packs[0][1], got[1]), "x")
        part = add(add(packs[0][0], got[0]), there)
        part = add(part[0], send(plan, part[1], "y"))
        part = reduce_z(plan, part)
        there = send(plan, part, "x")
        both = jnp.stack([part, there])
        both, grad_down = lax.optimization_barrier((both, grad_down))
        other = send(plan, both, "c")
        shapes = [(rows, width), (krows, width), (krows, width), (rows, width), (1, rows), (1, rows)]
        *results, gain_a, gain_m = unpack(plan, unpack_attention_kernel, place, both, other, shapes)
        return (
            output,
            grad_tokens,
            *[result.T for result in results],
            grad_gate.T,
            grad_up.T,
            grad_down.T,
            gain_a.reshape(rows),
            gain_m.reshape(rows),
        )
    else:

        def total(value):
            part = lax.psum_scatter(value.astype(F32), "fsdp", scatter_dimension=0, tiled=True)
            return lax.psum(part, "dp")

        both = grads[0][0][0].reshape(hidden, 2 * width)
        main, half = plan.main, 2 * plan.main + HEAD_SIZE
        grad_gate = total(jnp.concatenate([both[:, :main], both[:, 2 * main : half]], 1)).T
        grad_up = total(jnp.concatenate([both[:, main : 2 * main], both[:, half:]], 1)).T
        grad_down = total(grads[0][1][0].reshape(width, hidden)).T
        whole = packs[0].reshape(2, width + plan.kv, lanes)
        one = jnp.concatenate([total(whole[0, :width]), total(whole[0, width:])], 0)
        two = jnp.concatenate([total(whole[1, : plan.kv]), total(whole[1, plan.kv :])], 0)
        rows, krows = width // plan.fsdp, plan.kv // plan.fsdp
    return (
        output,
        grad_tokens,
        one[:rows, :width].T,
        one[rows:, :width].T,
        two[:krows, :width].T,
        two[krows:, :width].T,
        grad_gate,
        grad_up,
        grad_down,
        one[:rows, width],
        one[:rows, width + 1],
    )


def solution(mesh):
    rows = P(("dp", "fsdp"), None)
    cols = P(None, "fsdp")
    one = P("fsdp")

    def run(*args):
        plan = Plan(mesh, args[0].shape[1], args[8].shape[0])
        step = jax.shard_map(
            functools.partial(layer, plan),
            mesh=mesh,
            in_specs=(rows, rows) + (cols,) * 7 + (one, one),
            out_specs=(rows, rows) + (cols,) * 7 + (one, one),
            check_vma=False,
        )
        return step(*args)

    return run
```
